32 devices in a mesh: group: 4 (over x, core), member: 8 (over z, y).
Axes of the slice: x: 2, y: 2, z: 4, core: 2. Of those that a mesh axis runs over, the one named last changes fastest.
Arguments:
- right_side: float32 [32, 256, 4096], P(None, 'group', 'member'), may hold values from -8 to 8
- diagonal: float32 [256, 4096], P('group', 'member'), may hold values from 0.02 to 1
- face_weight: float32 [2, 256, 4096], P(None, 'group', 'member'), may hold values from 0.5 to 2
- aggregation: int32 [256, 4096], P('group', 'member'), may hold values from 0 to 127, as said below
Outputs:
- solution_field: float32 [32, 256, 4096], P(None, 'group', 'member')
The draws below stay inside these ranges and needn't reach their ends.
Inputs may be any that keep to these rules, and one draw needn't show every extreme that they name: `aggregation`: each cell names one aggregate of its own device block; the aggregates are irregular patches.
All inputs are finite; a program needn't handle non-finite values.
Results may differ from the reference program's by a relative error of at most 0.0003.
Values sent between devices are 32-bit elements; how exact they have to be, the bound alone decides.
A program may use at most 128 MiB of HBM per device.

```python
import math
import jax
import jax.numpy as jnp
from jax import lax

R = 32
CX = 64
CY = 512
AGG = 128
PRE = 2
POST = 2
CHEB = 6
NX = 256
NY = 4096
N_GROUP = 4
N_MEMBER = 8


def draw_aggregation(key, part):
    xs = lax.broadcasted_iota(jnp.int32, (NX, NY), 0)
    ys = lax.broadcasted_iota(jnp.int32, (NX, NY), 1)
    local_x = xs % CX
    local_y = ys % CY
    key_x, key_y = jax.random.split(jax.random.fold_in(key, 17))
    off_x = jax.random.randint(key_x, (NX, NY), -1, 2)
    off_y = jax.random.randint(key_y, (NX, NY), -2, 3)
    near_x = jnp.clip(local_x + off_x, 0, CX - 1)
    near_y = jnp.clip(local_y + off_y, 0, CY - 1)
    splits = min(CX, max(1, AGG * 4 // CY))
    height = max(1, CY * splits // AGG)
    tile = near_y // height * splits + near_x * splits // CX
    block = xs // CX * 3 + ys // CY * 7
    return ((tile * 37 + block * 11) % AGG).astype(jnp.int32)


def shard_levels(key, extent, cuts, smallest, high):
    gain, own = 1.0, jax.random.fold_in(key, 6)
    for axis_at, blocks in cuts:
        draws = jnp.exp(jax.random.uniform(jax.random.fold_in(own, axis_at), (blocks,), jnp.float32, smallest / len(cuts), high / len(cuts)))
        gain = gain * jnp.repeat(draws, extent[axis_at] // blocks).reshape([-1 if axis == axis_at else 1 for axis in range(len(extent))])
    return gain


def scatter_about(own_key, dims, deviation, limit, cuts=(), kind=jnp.bfloat16):
    entries = jax.random.normal(own_key, dims, jnp.float32) * deviation
    if len(cuts) > 0:
        entries = shard_levels(own_key, dims, cuts, -0.22, 0.18) * entries
    return jnp.clip(entries, min=-limit, max=limit).astype(kind)


def setup_inputs(seed: int = 0) -> dict:
    streams_of = jax.random.split(jax.random.key(seed), 5)
    right_side = scatter_about(streams_of[0], (R, NX, NY), 1.0, 8.0, ((1, 4), (2, 8)), jnp.float32)
    diagonal = jnp.clip(jnp.exp(math.log(1.0) - 3.912023 * jax.random.uniform(streams_of[1], (NX, NY), jnp.float32) ** shard_levels(streams_of[1], (NX, NY), ((0, 4), (1, 8)), -0.2, 0.2)), 0.02, 1.0)
    face_weight = jnp.clip(jnp.exp(math.log(2.0) - 1.3862944 * jax.random.uniform(streams_of[2], (2, NX, NY), jnp.float32) ** shard_levels(streams_of[2], (2, NX, NY), ((1, 4), (2, 8)), -0.2, 0.2)), 0.5, 2.0)
    aggregation = draw_aggregation(jax.random.fold_in(streams_of[4], 71), 0)
    return dict(right_side=right_side, diagonal=diagonal, face_weight=face_weight, aggregation=aggregation)


OMEGA = 0.8
RATIO = 30.0
HIGH_LEVEL = lax.Precision.HIGHEST


def lower_faces(wx, wy):
    wx_low = jnp.pad(wx, ((1, 0), (0, 0)))[:-1, :]
    wy_low = jnp.pad(wy, ((0, 0), (1, 0)))[:, :-1]
    return wx_low, wy_low


def stencil(field, diagf, wx, wy):
    wx_low, wy_low = lower_faces(wx, wy)
    padded = jnp.pad(field, ((0, 0), (1, 1), (1, 1)))
    beside = wx * padded[:, 2:, 1:-1] + wx_low * padded[:, :-2, 1:-1]
    beside = beside + wy * padded[:, 1:-1, 2:] + wy_low * padded[:, 1:-1, :-2]
    return diagf * field - beside


def smooth(field, rhs, diagf, wx, wy):
    return field + OMEGA * (rhs - stencil(field, diagf, wx, wy)) / diagf


def chebyshev(rhs, matvec, lmax):
    lmin = lmax / RATIO
    theta = (lmax + lmin) / 2.0
    delta = (lmax - lmin) / 2.0
    sigma = theta / delta
    rho = 1.0 / sigma
    sol = jnp.zeros_like(rhs)
    resid = rhs
    direc = rhs / theta
    for step in range(CHEB):
        sol = sol + direc
        if step + 1 < CHEB:
            resid = resid - matvec(direc)
            rho_new = 1.0 / (2.0 * sigma - rho)
            direc = rho_new * rho * direc + (2.0 * rho_new / delta) * resid
            rho = rho_new
    return sol


def coarse_product(input_vector, block_diagonal, block_lower):
    zero_vec = jnp.zeros_like(input_vector[:1])
    prior_columns = jnp.concatenate([zero_vec, input_vector[:-1]], axis=0)
    upper_band = jnp.einsum("fwg,fge->fwe", input_vector, block_lower, precision=HIGH_LEVEL)
    next_weight = jnp.concatenate([upper_band[1:], zero_vec], axis=0)
    return jnp.einsum("ioc,iqc->ioq", input_vector, block_diagonal, precision=HIGH_LEVEL) + jnp.einsum("ioc,iqc->ioq", prior_columns, block_lower, precision=HIGH_LEVEL) + next_weight


def bound_of(block_diagonal, block_lower):
    row_d = jnp.sum(jnp.abs(block_diagonal), axis=2)
    row_l = jnp.sum(jnp.abs(block_lower), axis=2)
    col_l = jnp.sum(jnp.abs(block_lower), axis=1)
    col_next = jnp.concatenate([col_l[1:], jnp.zeros_like(col_l[:1])], axis=0)
    return jnp.max(row_d + row_l + col_next)


def group_correction(args):
    agg_g, diag_g, wx_g, wy_g, resid_g = args
    labels = jnp.arange(AGG, dtype=jnp.int32)

    def per_block(block_args):
        agg_b, diag_b, wx_b, wy_b, resid_b = block_args
        onehot = (agg_b[None, :, :] == labels[:, None, None]).astype(jnp.float32)
        applied = stencil(onehot, diag_b, wx_b, wy_b)
        block_diagonal = jnp.einsum("axy,bxy->ab", onehot, applied, precision=HIGH_LEVEL)
        rhs_b = jnp.einsum("rxy,axy->ra", resid_b, onehot, precision=HIGH_LEVEL)
        return block_diagonal, rhs_b

    block_diagonal, coarse_rhs = lax.map(per_block, (agg_g, diag_g, wx_g, wy_g, resid_g))
    tops = agg_g[:, :, -1] + 1
    prevs = jnp.concatenate([jnp.zeros_like(tops[:1]), tops[:-1]], axis=0)
    last_weight = wy_g[:, :, -1]
    prev_weight = jnp.concatenate([jnp.zeros_like(last_weight[:1]), last_weight[:-1]], axis=0)
    prev_hot = (prevs[:, :, None] == (labels + 1)[None, None, :]).astype(jnp.float32)
    bottom_hot = (agg_g[:, :, 0][:, :, None] == labels[None, None, :]).astype(jnp.float32)
    block_lower = -jnp.einsum("mxa,mxb->mab", bottom_hot * prev_weight[:, :, None], prev_hot, precision=HIGH_LEVEL)
    lmax = bound_of(block_diagonal, block_lower)
    sol = chebyshev(coarse_rhs, lambda v: coarse_product(v, block_diagonal, block_lower), lmax)

    def expand(block_args):
        agg_b, sol_b = block_args
        onehot = (agg_b[None, :, :] == labels[:, None, None]).astype(jnp.float32)
        return jnp.einsum("ra,axy->rxy", sol_b, onehot, precision=HIGH_LEVEL)

    return lax.map(expand, (agg_g, sol))


def reference(right_side, diagonal, face_weight, aggregation):
    wx = face_weight[0]
    wy = face_weight[1]
    wx_low, wy_low = lower_faces(wx, wy)
    diagf = diagonal + wx + wy + wx_low + wy_low
    field = OMEGA * right_side / diagf
    for step in range(PRE - 1):
        field = smooth(field, right_side, diagf, wx, wy)
    resid = right_side - stencil(field, diagf, wx, wy)
    agg4 = aggregation.reshape(N_GROUP, CX, N_MEMBER, CY).transpose(0, 2, 1, 3)
    diag4 = diagf.reshape(N_GROUP, CX, N_MEMBER, CY).transpose(0, 2, 1, 3)
    wx4 = wx.reshape(N_GROUP, CX, N_MEMBER, CY).transpose(0, 2, 1, 3)
    wy4 = wy.reshape(N_GROUP, CX, N_MEMBER, CY).transpose(0, 2, 1, 3)
    resid5 = resid.reshape(R, N_GROUP, CX, N_MEMBER, CY).transpose(1, 3, 0, 2, 4)
    corr = lax.map(group_correction, (agg4, diag4, wx4, wy4, resid5))
    corr = corr.transpose(2, 0, 3, 1, 4).reshape(R, NX, NY)
    field = field + corr
    for step in range(POST):
        field = smooth(field, right_side, diagf, wx, wy)
    return field
```

```python
import functools

import jax
import jax.numpy as jnp
from jax import lax
from jax.experimental import pallas as pl
from jax.experimental.pallas import tpu as pltpu
from jax.sharding import PartitionSpec as P

AGG = 128
POST = 2
CHEB = 6
OMEGA = 0.8
RATIO = 30.0
LANES = 128
MESH = pl.DeviceIdType.MESH
F32 = jnp.float32
BF16 = jnp.bfloat16
NT = (((1,), (1,)), ((), ()))


def passed_along(value, axis, steps):
    count = lax.axis_size(axis)
    initial, last = (max(0, -steps), min(count, count - steps))
    return lax.ppermute(value, axis, [(source, source + steps) for source in range(initial, last)])


def split(value):
    high = value.astype(BF16)
    return high, (value - high.astype(F32)).astype(BF16)


def coarse_kernel(rows, cell_ref, edge_ref, w_ref, acc):
    step = pl.program_id(0)

    @pl.when(step == 0)
    def _():
        acc[...] = jnp.zeros_like(acc)

    width = cell_ref.shape[2]
    label = lax.broadcasted_iota(jnp.int32, (AGG, width), 0).astype(F32)
    total = jnp.zeros(acc.shape, F32)
    for x in range(rows):
        cell = cell_ref[x]
        own = label == cell[0:1]
        hot = jnp.where(own, 1.0, 0.0).astype(BF16)
        value = jnp.where(own, cell[3:4], 0.0)
        value = value - jnp.where(label == cell[1:2], cell[4:5], 0.0)
        value = value - jnp.where(label == cell[2:3], cell[5:6], 0.0)
        high, low = split(value)
        both = jnp.concatenate([high, low], axis=0)
        total = total + lax.dot_general(hot, both, NT, preferred_element_type=F32)
    acc[...] += total

    @pl.when(step == pl.num_programs(0) - 1)
    def _():
        half = acc[:, :AGG] + acc[:, AGG:]
        w_ref[0:AGG] = half + half.T
        edge = edge_ref[...]
        lab = lax.broadcasted_iota(jnp.int32, (AGG, LANES), 0).astype(F32)

        def lower(first, second, weight):
            left = jnp.where(lab == edge[first:first + 1], edge[weight:weight + 1], 0.0)
            right = jnp.where(lab == edge[second:second + 1], 1.0, 0.0)
            return -lax.dot_general(
                left, right, NT, precision=lax.Precision.HIGHEST, preferred_element_type=F32
            )

        w_ref[AGG:2 * AGG] = lower(0, 1, 2)
        w_ref[2 * AGG:3 * AGG] = lower(4, 3, 5)


def cycle_kernel(
    n_group, n_member, rhs_ref, coef_ref, w_ref, out_ref,
    b, f, g, h, col_send, col_recv, dir_send, dir_recv, lm_send, lm_recv,
    halo_ssem, halo_rsem, dir_ssem, dir_rsem, lm_ssem, lm_rsem,
):
    rows, n_rhs, width = rhs_ref.shape
    tiles = width // LANES
    gi = lax.axis_index("group")
    mi = lax.axis_index("member")
    g_up, g_down = lax.rem(gi + 1, n_group), lax.rem(gi + n_group - 1, n_group)
    m_up, m_down = lax.rem(mi + 1, n_member), lax.rem(mi + n_member - 1, n_member)

    barrier = pltpu.get_barrier_semaphore()
    for peer in (g_up, g_down):
        pl.semaphore_signal(barrier, inc=1, device_id=(peer, mi), device_id_type=MESH)
    for off in range(1, n_member):
        peer = lax.rem(mi + off, n_member)
        pl.semaphore_signal(barrier, inc=1, device_id=(gi, peer), device_id_type=MESH)

    lane = lax.broadcasted_iota(jnp.int32, (n_rhs, LANES), 1)
    label = lax.broadcasted_iota(jnp.int32, (AGG, width), 0).astype(F32)

    def remote(src, dst, ssem, rsem, target):
        return pltpu.make_async_remote_copy(
            src_ref=src, dst_ref=dst, send_sem=ssem, recv_sem=rsem,
            device_id=target, device_id_type=MESH,
        )

    def exchange(phase, buf):
        plan = (
            (buf.at[rows], buf.at[0], (g_up, mi)),
            (buf.at[1], buf.at[rows + 1], (g_down, mi)),
            (col_send.at[phase, 0], col_recv.at[phase, 0], (gi, m_up)),
            (col_send.at[phase, 1], col_recv.at[phase, 1], (gi, m_down)),
        )
        copies = [
            remote(s, d, halo_ssem.at[phase, i], halo_rsem.at[phase, i], t)
            for i, (s, d, t) in enumerate(plan)
        ]
        for copy in copies:
            copy.start()
        return copies

    def finish(copies):
        for copy in copies:
            copy.wait()

    def pack(x, value, carry):
        last, first = carry
        last = jnp.where(lane == x + 1, pltpu.roll(value[:, width - LANES:], x + 2, 1), last)
        first = jnp.where(lane == x, pltpu.roll(value[:, :LANES], x, 1), first)
        return last, first

    def store_columns(phase, carry):
        col_send[phase, 0] = carry[0]
        col_send[phase, 1] = carry[1]

    empty = (jnp.zeros((n_rhs, LANES), F32), jnp.zeros((n_rhs, LANES), F32))

    def neighbours(phase, buf, x, coef):
        cur = buf[x + 1]
        prev_t = pltpu.roll(col_recv[phase, 0], 127 - x, 1)
        back_t = pltpu.roll(col_recv[phase, 1], 127 - x, 1)
        parts = [cur[:, k * LANES:(k + 1) * LANES] for k in range(tiles)]
        right = [prev_t] + [pltpu.roll(p, 1, 1) for p in parts]
        left = [pltpu.roll(p, LANES - 1, 1) for p in parts] + [back_t]
        low = [jnp.where(lane == 0, right[k], right[k + 1]) for k in range(tiles)]
        high = [jnp.where(lane == LANES - 1, left[k + 1], left[k]) for k in range(tiles)]
        low = jnp.concatenate(low, axis=1)
        high = jnp.concatenate(high, axis=1)
        total = coef[0:1] * buf[x + 2] + coef[1:2] * buf[x]
        return cur, total + coef[2:3] * high + coef[3:4] * low

    def hot_of(coef):
        return jnp.where(label == coef[6:7], 1.0, 0.0).astype(BF16)

    def scale(x, carry):
        value = rhs_ref[x] * coef_ref[x][4:5]
        b[x + 1] = value
        return pack(x, value, carry)

    store_columns(0, lax.fori_loop(0, rows, scale, empty, unroll=2))
    w = w_ref[...]
    lm = jnp.sum(jnp.abs(w), axis=0, keepdims=True)
    lm_send[...] = jnp.broadcast_to(lm, lm_send.shape)
    pl.semaphore_wait(barrier, n_member + 1)

    first = exchange(0, b)
    lm_copies = []
    for off in range(1, n_member):
        peer = lax.rem(mi + off, n_member)
        copy = remote(
            lm_send, lm_recv.at[off - 1], lm_ssem.at[off - 1], lm_rsem.at[off - 1], (gi, peer)
        )
        copy.start()
        lm_copies.append(copy)
    w_high, w_low = split(w)
    finish(first)

    def pre(x, carry):
        cur, total = neighbours(0, b, x, coef_ref[x])
        value = (2.0 - OMEGA) * cur + total
        f[x + 1] = value
        return pack(x, value, carry)

    store_columns(1, lax.fori_loop(0, rows, pre, empty, unroll=2))
    finish(exchange(1, f))

    def restrict(x, carry):
        coef = coef_ref[x]
        cur, total = neighbours(1, f, x, coef)
        resid = (b[x + 1] - OMEGA * cur + total) * coef[5:6]
        high, low = split(resid)
        both = jnp.concatenate([high, low], axis=0)
        return carry + lax.dot_general(both, hot_of(coef), NT, preferred_element_type=F32)

    sums = lax.fori_loop(0, rows, restrict, jnp.zeros((2 * n_rhs, AGG), F32), unroll=4)
    resid = sums[:n_rhs] + sums[n_rhs:]

    for copy in lm_copies:
        copy.wait()
    lm8 = lm_send[...]
    for off in range(1, n_member):
        lm8 = jnp.maximum(lm8, lm_recv[off - 1])
    lmax = jnp.max(lm8[0:1], axis=1, keepdims=True)
    lmin = lmax / RATIO
    theta = (lmax + lmin) / 2.0
    delta = (lmax - lmin) / 2.0
    sigma = theta / delta
    rho = 1.0 / sigma
    direc = resid / theta
    sol = jnp.zeros_like(resid)
    for step in range(CHEB):
        if step + 1 < CHEB:
            dir_send[step] = direc
            copies = [
                remote(
                    dir_send.at[step], dir_recv.at[step, i],
                    dir_ssem.at[step, i], dir_rsem.at[step, i], (gi, peer),
                )
                for i, peer in enumerate((m_up, m_down))
            ]
            for copy in copies:
                copy.start()
            sol = sol + direc
            rho_new = 1.0 / (2.0 * sigma - rho)
            finish(copies)
            vec = jnp.concatenate([direc, dir_recv[step, 0], dir_recv[step, 1]], axis=1)
            v_high, v_low = split(vec)
            both = jnp.concatenate([v_high, v_low], axis=0)
            prod = jnp.dot(both, w_high, preferred_element_type=F32)
            prod = prod[:n_rhs] + prod[n_rhs:]
            prod = prod + jnp.dot(v_high, w_low, preferred_element_type=F32)
            resid = resid - prod
            direc = rho_new * rho * direc + (2.0 * rho_new / delta) * resid
            rho = rho_new
        else:
            sol = sol + direc

    e_high, e_low = split(sol)
    e_both = jnp.concatenate([e_high, e_low], axis=0)

    def prolong(x, carry):
        spread = jnp.dot(e_both, hot_of(coef_ref[x]), preferred_element_type=F32)
        value = f[x + 1] + spread[:n_rhs] + spread[n_rhs:]
        g[x + 1] = value
        return pack(x, value, carry)

    store_columns(2, lax.fori_loop(0, rows, prolong, empty, unroll=4))
    finish(exchange(2, g))

    def post(x, carry):
        cur, total = neighbours(2, g, x, coef_ref[x])
        value = b[x + 1] + (1.0 - OMEGA) * cur + total
        h[x + 1] = value
        return pack(x, value, carry)

    store_columns(3, lax.fori_loop(0, rows, post, empty, unroll=2))
    finish(exchange(3, h))

    def final(x, carry):
        cur, total = neighbours(3, h, x, coef_ref[x])
        out_ref[x] = b[x + 1] + (1.0 - OMEGA) * cur + total
        return carry

    lax.fori_loop(0, rows, final, 0, unroll=2)


def local(right_side, diagonal, face_weight, aggregation):
    n_group, n_member = lax.axis_size("group"), lax.axis_size("member")
    n_rhs, rows, width = right_side.shape
    wx = face_weight[0]
    wy = face_weight[1]
    agg = aggregation.astype(F32)
    low_row = passed_along(wx[-1:, :], "group", 1)
    forward = passed_along(jnp.stack([agg[:, -1] + 1.0, wy[:, -1]]), "member", 1)
    backward = passed_along(agg[:, 0] + 1.0, "member", -1)
    below_weight = forward[1]
    wx_low = jnp.concatenate([low_row, wx[:-1, :]], axis=0)
    wy_low = jnp.concatenate([below_weight[:, None], wy[:, :-1]], axis=1)
    diagf = diagonal + wx + wy + wx_low + wy_low
    xs = lax.broadcasted_iota(jnp.int32, (rows, width), 0)
    ys = lax.broadcasted_iota(jnp.int32, (rows, width), 1)
    last_x = (lax.axis_index("group") == n_group - 1) & (xs == rows - 1)
    last_y = (lax.axis_index("member") == n_member - 1) & (ys == width - 1)
    q = OMEGA / diagf
    coef = jnp.stack(
        [
            jnp.where(last_x, 0.0, q * wx), q * wx_low, jnp.where(last_y, 0.0, q * wy), q * wy_low,
            q, diagf * (1.0 / OMEGA), agg, agg,
        ],
        axis=1,
    )
    agg_x = jnp.concatenate([agg[1:], agg[-1:]], axis=0)
    agg_y = jnp.concatenate([agg[:, 1:], agg[:, -1:]], axis=1)
    cell = jnp.stack(
        [
            agg, agg_x, agg_y, 0.5 * diagf,
            jnp.where(xs == rows - 1, 0.0, wx), jnp.where(ys == width - 1, 0.0, wy), agg, agg,
        ],
        axis=1,
    )
    edge = jnp.stack(
        [
            forward[0] - 1.0, agg[:, 0], below_weight, agg[:, -1], backward - 1.0, wy[:, -1],
            below_weight, below_weight,
        ]
    )
    edge = jnp.pad(edge, ((0, 0), (0, LANES - rows)), constant_values=-1.0)

    block = 8
    w = pl.pallas_call(
        functools.partial(coarse_kernel, block),
        grid=(rows // block,),
        out_shape=jax.ShapeDtypeStruct((3 * AGG, AGG), F32),
        in_specs=[
            pl.BlockSpec((block, 8, width), lambda i: (i, 0, 0)),
            pl.BlockSpec((8, LANES), lambda i: (0, 0)),
        ],
        out_specs=pl.BlockSpec((3 * AGG, AGG), lambda i: (0, 0)),
        scratch_shapes=[pltpu.VMEM((AGG, 2 * AGG), F32)],
    )(cell, edge)

    padded = pltpu.VMEM((rows + 2, n_rhs, width), F32)
    dma = pltpu.SemaphoreType.DMA
    vmem = pl.BlockSpec(memory_space=pltpu.VMEM)
    out = pl.pallas_call(
        functools.partial(cycle_kernel, n_group, n_member),
        out_shape=jax.ShapeDtypeStruct((rows, n_rhs, width), F32),
        in_specs=[vmem] * 3,
        out_specs=vmem,
        scratch_shapes=[
            padded, padded, padded, padded,
            pltpu.VMEM((4, 2, n_rhs, LANES), F32),
            pltpu.VMEM((4, 2, n_rhs, LANES), F32),
            pltpu.VMEM((CHEB - 1, n_rhs, AGG), F32),
            pltpu.VMEM((CHEB - 1, 2, n_rhs, AGG), F32),
            pltpu.VMEM((8, AGG), F32),
            pltpu.VMEM((n_member - 1, 8, AGG), F32),
            dma((4, 4)), dma((4, 4)),
            dma((CHEB - 1, 2)), dma((CHEB - 1, 2)),
            dma((n_member - 1,)), dma((n_member - 1,)),
        ],
        compiler_params=pltpu.CompilerParams(
            collective_id=0, has_side_effects=True, vmem_limit_bytes=48 * 1024 * 1024
        ),
    )(right_side.transpose(1, 0, 2), coef, w)
    return out.transpose(1, 0, 2)


def solution(mesh):
    placed = (
        P(None, "group", "member"),
        P("group", "member"),
        P(None, "group", "member"),
        P("group", "member"),
    )
    return jax.shard_map(
        local, mesh=mesh, in_specs=placed, out_specs=P(None, "group", "member"), check_vma=False
    )
```

```python
import functools

import jax
import jax.numpy as jnp
from jax import lax
from jax.experimental import pallas as pl
from jax.experimental.pallas import tpu as pltpu
from jax.sharding import PartitionSpec as P

AGG = 128
POST = 2
CHEB = 6
OMEGA = 0.8
RATIO = 30.0
LANES = 128
MESH = pl.DeviceIdType.MESH
F32 = jnp.float32
BF16 = jnp.bfloat16
NT = (((1,), (1,)), ((), ()))


def split(value):
    high = value.astype(BF16)
    return high, (value - high.astype(F32)).astype(BF16)


AX, AX_LOW, AY, AY_LOW, Q, Q_INV, LABEL, LABEL_X, LABEL_Y, WX, WY, HALF = range(12)
D_BLOCK = 4


def cycle_kernel(
    n_group, n_member, rhs_hbm, diag_ref, face_ref, agg_ref, out_ref,
    rhs, cf, acc, low_row_ref, below_w_ref, below_a_ref, above_a_ref,
    b, f, g, h, col_send, col_recv, dir_send, dir_recv, lm_send, lm_recv,
    rhs_sem, edge_ssem, edge_rsem, halo_ssem, halo_rsem, dir_ssem, dir_rsem, lm_ssem, lm_rsem,
):
    rows, n_rhs, width = rhs.shape
    tiles = width // LANES
    gi = lax.axis_index("group")
    mi = lax.axis_index("member")
    g_up, g_down = lax.rem(gi + 1, n_group), lax.rem(gi + n_group - 1, n_group)
    m_up, m_down = lax.rem(mi + 1, n_member), lax.rem(mi + n_member - 1, n_member)

    def fetch(x):
        return pltpu.make_async_copy(rhs_hbm.at[:, x, :], rhs.at[x], rhs_sem.at[x])

    def start_fetch(x, carry):
        fetch(x).start()
        return carry

    lax.fori_loop(0, rows, start_fetch, 0)

    barrier = pltpu.get_barrier_semaphore()
    for peer in (g_up, g_down):
        pl.semaphore_signal(barrier, inc=1, device_id=(peer, mi), device_id_type=MESH)
    for off in range(1, n_member):
        peer = lax.rem(mi + off, n_member)
        pl.semaphore_signal(barrier, inc=1, device_id=(gi, peer), device_id_type=MESH)

    lane = lax.broadcasted_iota(jnp.int32, (n_rhs, LANES), 1)
    label = lax.broadcasted_iota(jnp.int32, (AGG, width), 0).astype(F32)

    def remote(src, dst, ssem, rsem, target):
        return pltpu.make_async_remote_copy(
            src_ref=src, dst_ref=dst, send_sem=ssem, recv_sem=rsem,
            device_id=target, device_id_type=MESH,
        )

    def exchange(phase, buf):
        plan = (
            (buf.at[rows], buf.at[0], (g_up, mi)),
            (buf.at[1], buf.at[rows + 1], (g_down, mi)),
            (col_send.at[phase, 0], col_recv.at[phase, 0], (gi, m_up)),
            (col_send.at[phase, 1], col_recv.at[phase, 1], (gi, m_down)),
        )
        copies = [
            remote(s, d, halo_ssem.at[phase, i], halo_rsem.at[phase, i], t)
            for i, (s, d, t) in enumerate(plan)
        ]
        for copy in copies:
            copy.start()
        return copies

    def finish(copies):
        for copy in copies:
            copy.wait()

    def pack(x, value, carry):
        last, first = carry
        last = jnp.where(lane == x + 1, pltpu.roll(value[:, width - LANES:], x + 2, 1), last)
        first = jnp.where(lane == x, pltpu.roll(value[:, :LANES], x, 1), first)
        return last, first

    def store_columns(phase, carry):
        col_send[phase, 0] = carry[0]
        col_send[phase, 1] = carry[1]

    empty = (jnp.zeros((n_rhs, LANES), F32), jnp.zeros((n_rhs, LANES), F32))

    def neighbours(phase, buf, x):
        cur = buf[x + 1]
        prev_t = pltpu.roll(col_recv[phase, 0], 127 - x, 1)
        back_t = pltpu.roll(col_recv[phase, 1], 127 - x, 1)
        parts = [cur[:, k * LANES:(k + 1) * LANES] for k in range(tiles)]
        right = [prev_t] + [pltpu.roll(p, 1, 1) for p in parts]
        left = [pltpu.roll(p, LANES - 1, 1) for p in parts] + [back_t]
        low = [jnp.where(lane == 0, right[k], right[k + 1]) for k in range(tiles)]
        high = [jnp.where(lane == LANES - 1, left[k + 1], left[k]) for k in range(tiles)]
        low = jnp.concatenate(low, axis=1)
        high = jnp.concatenate(high, axis=1)
        total = cf[AX, pl.ds(x, 1), :] * buf[x + 2] + cf[AX_LOW, pl.ds(x, 1), :] * buf[x]
        return cur, total + cf[AY, pl.ds(x, 1), :] * high + cf[AY_LOW, pl.ds(x, 1), :] * low

    def row(plane, x):
        return cf[plane, pl.ds(x, 1), :]

    def hot_of(x):
        return jnp.where(label == row(LABEL, x), 1.0, 0.0).astype(BF16)

    wx, wy, agg = face_ref[0], face_ref[1], agg_ref[...].astype(F32)
    xs = lax.broadcasted_iota(jnp.int32, (rows, width), 0)
    ys = lax.broadcasted_iota(jnp.int32, (rows, width), 1)
    wx_low = jnp.where(xs == 0, 0.0, pltpu.roll(wx, 1, 0))
    wy_low = jnp.where(ys == 0, 0.0, pltpu.roll(wy, 1, 1))
    own_diag = diag_ref[...] + wx + wy + wx_low + wy_low
    cf[LABEL] = agg
    cf[LABEL_X] = pltpu.roll(agg, rows - 1, 0)
    cf[LABEL_Y] = pltpu.roll(agg, width - 1, 1)
    cf[WX] = jnp.where(xs == rows - 1, 0.0, wx)
    cf[WY] = jnp.where(ys == width - 1, 0.0, wy)
    cf[HALF] = 0.5 * own_diag
    acc[...] = jnp.zeros_like(acc)

    pl.semaphore_wait(barrier, n_member + 1)
    edges = [
        remote(s, d, edge_ssem.at[i], edge_rsem.at[i], t)
        for i, (s, d, t) in enumerate((
            (face_ref.at[0, pl.ds(rows - 8, 8), :], low_row_ref, (g_up, mi)),
            (face_ref.at[1, :, pl.ds(width - LANES, LANES)], below_w_ref, (gi, m_up)),
            (agg_ref.at[:, pl.ds(width - LANES, LANES)], below_a_ref, (gi, m_up)),
            (agg_ref.at[:, pl.ds(0, LANES)], above_a_ref, (gi, m_down)),
        ))
    ]
    for copy in edges:
        copy.start()

    def pairs(block, carry):
        total = jnp.zeros(acc.shape, F32)
        for i in range(D_BLOCK):
            x = block * D_BLOCK + i
            own = label == row(LABEL, x)
            hot = jnp.where(own, 1.0, 0.0).astype(BF16)
            value = jnp.where(own, row(HALF, x), 0.0)
            value = value - jnp.where(label == row(LABEL_X, x), row(WX, x), 0.0)
            value = value - jnp.where(label == row(LABEL_Y, x), row(WY, x), 0.0)
            high, low = split(value)
            both = jnp.concatenate([high, low], axis=0)
            total = total + lax.dot_general(hot, both, NT, preferred_element_type=F32)
        acc[...] += total
        return carry

    blocks = rows // D_BLOCK
    early = blocks * 5 // 8
    lax.fori_loop(0, early, pairs, 0)
    finish(edges)

    low_row = jnp.where(gi > 0, low_row_ref[7:8, :], 0.0)
    below = jnp.where(mi > 0, below_w_ref[:, LANES - 1:], 0.0)
    wx_low = wx_low + jnp.where(xs == 0, low_row, 0.0)
    wy_low = wy_low + jnp.where(ys == 0, below, 0.0)
    diagf = diag_ref[...] + wx + wy + wx_low + wy_low
    q = OMEGA / diagf
    last_x = (xs == rows - 1) & (gi == n_group - 1)
    last_y = (ys == width - 1) & (mi == n_member - 1)
    cf[AX] = jnp.where(last_x, 0.0, q * wx)
    cf[AX_LOW] = q * wx_low
    cf[AY] = jnp.where(last_y, 0.0, q * wy)
    cf[AY_LOW] = q * wy_low
    cf[Q] = q
    cf[Q_INV] = diagf * (1.0 / OMEGA)

    def scale(x, carry):
        fetch(x).wait()
        value = rhs[x] * row(Q, x)
        b[x + 1] = value
        return pack(x, value, carry)

    store_columns(0, lax.fori_loop(0, rows, scale, empty, unroll=2))
    first = exchange(0, b)
    lax.fori_loop(early, blocks, pairs, 0)

    def dot_high(left, right):
        return jnp.dot(
            left, right, precision=lax.Precision.HIGHEST, preferred_element_type=F32
        )

    lab = lax.broadcasted_iota(jnp.int32, (rows, LANES), 1)

    def hot_column(column):
        return jnp.where(column == lab, 1.0, 0.0)

    first_hot = hot_column(agg_ref[:, 0:1])
    last_hot = hot_column(agg_ref[:, width - 1:])
    below_hot = hot_column(below_a_ref[:, LANES - 1:])
    above_hot = hot_column(above_a_ref[:, 0:1])
    above = jnp.where(mi < n_member - 1, face_ref[1, :, width - 1:], 0.0)
    half = acc[:, :AGG] + acc[:, AGG:]
    half = half + dot_high(first_hot.T, first_hot * (0.5 * below))
    own = label == row(LABEL, 0)
    low_sum = jnp.sum(jnp.where(own, low_row, 0.0), axis=1, keepdims=True)
    eye = lax.broadcasted_iota(jnp.int32, (AGG, AGG), 0)
    eye = eye == lax.broadcasted_iota(jnp.int32, (AGG, AGG), 1)
    half = half + jnp.where(eye, 0.5 * low_sum, 0.0)
    w = jnp.concatenate(
        [
            half + half.T,
            -dot_high(below_hot.T, first_hot * below),
            -dot_high(above_hot.T, last_hot * above),
        ],
        axis=0,
    )
    lm = jnp.sum(jnp.abs(w), axis=0, keepdims=True)
    lm_send[...] = jnp.broadcast_to(lm, lm_send.shape)
    lm_copies = []
    for off in range(1, n_member):
        peer = lax.rem(mi + off, n_member)
        copy = remote(
            lm_send, lm_recv.at[off - 1], lm_ssem.at[off - 1], lm_rsem.at[off - 1], (gi, peer)
        )
        copy.start()
        lm_copies.append(copy)
    w_high, w_low = split(w)
    finish(first)

    def pre(x, carry):
        cur, total = neighbours(0, b, x)
        value = (2.0 - OMEGA) * cur + total
        f[x + 1] = value
        return pack(x, value, carry)

    store_columns(1, lax.fori_loop(0, rows, pre, empty, unroll=2))
    finish(exchange(1, f))

    def restrict(x, carry):
        cur, total = neighbours(1, f, x)
        resid = (b[x + 1] - OMEGA * cur + total) * row(Q_INV, x)
        high, low = split(resid)
        both = jnp.concatenate([high, low], axis=0)
        return carry + lax.dot_general(both, hot_of(x), NT, preferred_element_type=F32)

    sums = lax.fori_loop(0, rows, restrict, jnp.zeros((2 * n_rhs, AGG), F32), unroll=4)
    resid = sums[:n_rhs] + sums[n_rhs:]

    for copy in lm_copies:
        copy.wait()
    lm8 = lm_send[...]
    for off in range(1, n_member):
        lm8 = jnp.maximum(lm8, lm_recv[off - 1])
    lmax = jnp.max(lm8[0:1], axis=1, keepdims=True)
    lmin = lmax / RATIO
    theta = (lmax + lmin) / 2.0
    delta = (lmax - lmin) / 2.0
    sigma = theta / delta
    rho = 1.0 / sigma
    direc = resid / theta
    sol = jnp.zeros_like(resid)
    for step in range(CHEB):
        if step + 1 < CHEB:
            dir_send[step] = direc
            copies = [
                remote(
                    dir_send.at[step], dir_recv.at[step, i],
                    dir_ssem.at[step, i], dir_rsem.at[step, i], (gi, peer),
                )
                for i, peer in enumerate((m_up, m_down))
            ]
            for copy in copies:
                copy.start()
            sol = sol + direc
            rho_new = 1.0 / (2.0 * sigma - rho)
            finish(copies)
            vec = jnp.concatenate([direc, dir_recv[step, 0], dir_recv[step, 1]], axis=1)
            v_high, v_low = split(vec)
            both = jnp.concatenate([v_high, v_low], axis=0)
            prod = jnp.dot(both, w_high, preferred_element_type=F32)
            prod = prod[:n_rhs] + prod[n_rhs:]
            prod = prod + jnp.dot(v_high, w_low, preferred_element_type=F32)
            resid = resid - prod
            direc = rho_new * rho * direc + (2.0 * rho_new / delta) * resid
            rho = rho_new
        else:
            sol = sol + direc

    e_high, e_low = split(sol)
    e_both = jnp.concatenate([e_high, e_low], axis=0)

    def prolong(x, carry):
        spread = jnp.dot(e_both, hot_of(x), preferred_element_type=F32)
        value = f[x + 1] + spread[:n_rhs] + spread[n_rhs:]
        g[x + 1] = value
        return pack(x, value, carry)

    store_columns(2, lax.fori_loop(0, rows, prolong, empty, unroll=4))
    finish(exchange(2, g))

    def post(x, carry):
        cur, total = neighbours(2, g, x)
        value = b[x + 1] + (1.0 - OMEGA) * cur + total
        h[x + 1] = value
        return pack(x, value, carry)

    store_columns(3, lax.fori_loop(0, rows, post, empty, unroll=2))
    finish(exchange(3, h))

    def final(x, carry):
        cur, total = neighbours(3, h, x)
        out_ref[x] = b[x + 1] + (1.0 - OMEGA) * cur + total
        return carry

    lax.fori_loop(0, rows, final, 0, unroll=2)


def local(right_side, diagonal, face_weight, aggregation):
    n_group, n_member = lax.axis_size("group"), lax.axis_size("member")
    n_rhs, rows, width = right_side.shape
    padded = pltpu.VMEM((rows + 2, n_rhs, width), F32)
    dma = pltpu.SemaphoreType.DMA
    vmem = pl.BlockSpec(memory_space=pltpu.VMEM)
    out = pl.pallas_call(
        functools.partial(cycle_kernel, n_group, n_member),
        out_shape=jax.ShapeDtypeStruct((rows, n_rhs, width), F32),
        in_specs=[pl.BlockSpec(memory_space=pl.ANY), vmem, vmem, vmem],
        out_specs=vmem,
        scratch_shapes=[
            pltpu.VMEM((rows, n_rhs, width), F32),
            pltpu.VMEM((12, rows, width), F32),
            pltpu.VMEM((AGG, 2 * AGG), F32),
            pltpu.VMEM((8, width), F32),
            pltpu.VMEM((rows, LANES), F32),
            pltpu.VMEM((rows, LANES), jnp.int32),
            pltpu.VMEM((rows, LANES), jnp.int32),
            padded, padded, padded, padded,
            pltpu.VMEM((4, 2, n_rhs, LANES), F32),
            pltpu.VMEM((4, 2, n_rhs, LANES), F32),
            pltpu.VMEM((CHEB - 1, n_rhs, AGG), F32),
            pltpu.VMEM((CHEB - 1, 2, n_rhs, AGG), F32),
            pltpu.VMEM((8, AGG), F32),
            pltpu.VMEM((n_member - 1, 8, AGG), F32),
            dma((rows,)), dma((4,)), dma((4,)),
            dma((4, 4)), dma((4, 4)),
            dma((CHEB - 1, 2)), dma((CHEB - 1, 2)),
            dma((n_member - 1,)), dma((n_member - 1,)),
        ],
        compiler_params=pltpu.CompilerParams(
            collective_id=0, has_side_effects=True, vmem_limit_bytes=48 * 1024 * 1024
        ),
    )(right_side, diagonal, face_weight, aggregation)
    return out.transpose(1, 0, 2)


def solution(mesh):
    placed = (
        P(None, "group", "member"),
        P("group", "member"),
        P(None, "group", "member"),
        P("group", "member"),
    )
    return jax.shard_map(
        local, mesh=mesh, in_specs=placed, out_specs=P(None, "group", "member"), check_vma=False
    )
```

```python
import functools

import jax
import jax.numpy as jnp
from jax import lax
from jax.experimental import pallas as pl
from jax.experimental.pallas import tpu as pltpu
from jax.sharding import PartitionSpec as P

AGG = 128
POST = 2
CHEB = 6
OMEGA = 0.8
RATIO = 30.0
LANES = 128
MESH = pl.DeviceIdType.MESH
F32 = jnp.float32
BF16 = jnp.bfloat16
NT = (((1,), (1,)), ((), ()))


def split(value):
    high = value.astype(BF16)
    return high, (value - high.astype(F32)).astype(BF16)


AX, AX_LOW, AY, AY_LOW, Q, Q_INV, LABEL, LABEL_X, LABEL_Y, WX, WY, HALF = range(12)
D_BLOCK = 4


def cycle_kernel(
    n_group, n_member, rhs_hbm, diag_ref, face_ref, agg_ref, out_ref,
    rhs, cf, acc, low_row_ref, below_w_ref, below_a_ref, above_a_ref,
    b, f, g, h, col_send, col_recv, dir_send, dir_recv, lm_send, lm_recv,
    rhs_sem, edge_ssem, edge_rsem, halo_ssem, halo_rsem, dir_ssem, dir_rsem, lm_ssem, lm_rsem,
):
    rows, n_rhs, width = rhs.shape
    tiles = width // LANES
    gi = lax.axis_index("group")
    mi = lax.axis_index("member")
    g_up, g_down = lax.rem(gi + 1, n_group), lax.rem(gi + n_group - 1, n_group)
    m_up, m_down = lax.rem(mi + 1, n_member), lax.rem(mi + n_member - 1, n_member)

    def fetch(x):
        return pltpu.make_async_copy(rhs_hbm.at[:, x, :], rhs.at[x], rhs_sem.at[x])

    def start_fetch(x, carry):
        fetch(x).start()
        return carry

    lax.fori_loop(0, rows, start_fetch, 0)

    barrier = pltpu.get_barrier_semaphore()
    for peer in (g_up, g_down):
        pl.semaphore_signal(barrier, inc=1, device_id=(peer, mi), device_id_type=MESH)
    for off in range(1, n_member):
        peer = lax.rem(mi + off, n_member)
        pl.semaphore_signal(barrier, inc=1, device_id=(gi, peer), device_id_type=MESH)

    lane = lax.broadcasted_iota(jnp.int32, (n_rhs, LANES), 1)
    label = lax.broadcasted_iota(jnp.int32, (AGG, width), 0).astype(F32)

    def remote(src, dst, ssem, rsem, target):
        return pltpu.make_async_remote_copy(
            src_ref=src, dst_ref=dst, send_sem=ssem, recv_sem=rsem,
            device_id=target, device_id_type=MESH,
        )

    def exchange(phase, buf):
        plan = (
            (buf.at[rows], buf.at[0], (g_up, mi)),
            (buf.at[1], buf.at[rows + 1], (g_down, mi)),
            (col_send.at[phase, 0], col_recv.at[phase, 0], (gi, m_up)),
            (col_send.at[phase, 1], col_recv.at[phase, 1], (gi, m_down)),
        )
        copies = [
            remote(s, d, halo_ssem.at[phase, i], halo_rsem.at[phase, i], t)
            for i, (s, d, t) in enumerate(plan)
        ]
        for copy in copies:
            copy.start()
        return copies

    started = []

    def finish(copies):
        for copy in copies:
            copy.wait_recv()
        started.extend(copies)

    def pack(x, value, carry):
        last, first = carry
        last = jnp.where(lane == x + 1, pltpu.roll(value[:, value.shape[1] - LANES:], x + 2, 1), last)
        first = jnp.where(lane == x, pltpu.roll(value[:, :LANES], x, 1), first)
        return last, first

    def store_columns(phase, carry):
        col_send[phase, 0] = carry[0]
        col_send[phase, 1] = carry[1]

    empty = (jnp.zeros((n_rhs, LANES), F32), jnp.zeros((n_rhs, LANES), F32))

    def neighbours(buf, x):
        cur = buf[x + 1]
        parts = [cur[:, k * LANES:(k + 1) * LANES] for k in range(tiles)]
        zero = jnp.zeros((n_rhs, LANES), F32)
        right = [zero] + [pltpu.roll(p, 1, 1) for p in parts]
        left = [pltpu.roll(p, LANES - 1, 1) for p in parts] + [zero]
        low = [jnp.where(lane == 0, right[k], right[k + 1]) for k in range(tiles)]
        high = [jnp.where(lane == LANES - 1, left[k + 1], left[k]) for k in range(tiles)]
        low = jnp.concatenate(low, axis=1)
        high = jnp.concatenate(high, axis=1)
        total = cf[AX, pl.ds(x, 1), :] * buf[x + 2] + cf[AX_LOW, pl.ds(x, 1), :] * buf[x]
        return cur, total + cf[AY, pl.ds(x, 1), :] * high + cf[AY_LOW, pl.ds(x, 1), :] * low

    def patch(phase, x):
        before = pltpu.roll(col_recv[phase, 0], 127 - x, 1)
        after = pltpu.roll(col_recv[phase, 1], 127 - x, 1)
        low = jnp.where(lane == 0, before, 0.0) * cf[AY_LOW, pl.ds(x, 1), :][:, :LANES]
        high = jnp.where(lane == LANES - 1, after, 0.0) * cf[AY, pl.ds(x, 1), :][:, width - LANES:]
        return low, high

    def sweep(phase, copies, body, dest, shift, unroll):
        def inner(x, carry):
            dest[x + shift] = body(x)
            return carry

        lax.fori_loop(1, rows - 1, inner, 0, unroll=unroll)
        finish(copies)
        inner(0, 0)
        inner(rows - 1, 0)

        def outer(x, carry):
            low, high = patch(phase, x)
            first = dest[x + shift, :, :LANES] + low
            last = dest[x + shift, :, width - LANES:] + high
            dest[x + shift, :, :LANES] = first
            dest[x + shift, :, width - LANES:] = last
            return pack(x, jnp.concatenate([first, last], axis=1), carry)

        return lax.fori_loop(0, rows, outer, empty, unroll=4)

    def row(plane, x):
        return cf[plane, pl.ds(x, 1), :]

    def hot_of(x):
        return jnp.where(label == row(LABEL, x), 1.0, 0.0).astype(BF16)

    wx, wy, agg = face_ref[0], face_ref[1], agg_ref[...].astype(F32)
    xs = lax.broadcasted_iota(jnp.int32, (rows, width), 0)
    ys = lax.broadcasted_iota(jnp.int32, (rows, width), 1)
    wx_low = jnp.where(xs == 0, 0.0, pltpu.roll(wx, 1, 0))
    wy_low = jnp.where(ys == 0, 0.0, pltpu.roll(wy, 1, 1))
    own_diag = diag_ref[...] + wx + wy + wx_low + wy_low
    cf[LABEL] = agg
    cf[LABEL_X] = pltpu.roll(agg, rows - 1, 0)
    cf[LABEL_Y] = pltpu.roll(agg, width - 1, 1)
    cf[WX] = jnp.where(xs == rows - 1, 0.0, wx)
    cf[WY] = jnp.where(ys == width - 1, 0.0, wy)
    cf[HALF] = 0.5 * own_diag
    acc[...] = jnp.zeros_like(acc)

    pl.semaphore_wait(barrier, n_member + 1)
    edges = [
        remote(s, d, edge_ssem.at[i], edge_rsem.at[i], t)
        for i, (s, d, t) in enumerate((
            (face_ref.at[0, pl.ds(rows - 8, 8), :], low_row_ref, (g_up, mi)),
            (face_ref.at[1, :, pl.ds(width - LANES, LANES)], below_w_ref, (gi, m_up)),
            (agg_ref.at[:, pl.ds(width - LANES, LANES)], below_a_ref, (gi, m_up)),
            (agg_ref.at[:, pl.ds(0, LANES)], above_a_ref, (gi, m_down)),
        ))
    ]
    for copy in edges:
        copy.start()

    def pairs(block, carry):
        total = jnp.zeros(acc.shape, F32)
        for i in range(D_BLOCK):
            x = block * D_BLOCK + i
            own = label == row(LABEL, x)
            hot = jnp.where(own, 1.0, 0.0).astype(BF16)
            value = jnp.where(own, row(HALF, x), 0.0)
            value = value - jnp.where(label == row(LABEL_X, x), row(WX, x), 0.0)
            value = value - jnp.where(label == row(LABEL_Y, x), row(WY, x), 0.0)
            high, low = split(value)
            both = jnp.concatenate([high, low], axis=0)
            total = total + lax.dot_general(hot, both, NT, preferred_element_type=F32)
        acc[...] += total
        return carry

    blocks = rows // D_BLOCK
    early = blocks * 5 // 8
    lax.fori_loop(0, early, pairs, 0)
    finish(edges)

    low_row = jnp.where(gi > 0, low_row_ref[7:8, :], 0.0)
    below = jnp.where(mi > 0, below_w_ref[:, LANES - 1:], 0.0)
    wx_low = wx_low + jnp.where(xs == 0, low_row, 0.0)
    wy_low = wy_low + jnp.where(ys == 0, below, 0.0)
    diagf = diag_ref[...] + wx + wy + wx_low + wy_low
    q = OMEGA / diagf
    last_x = (xs == rows - 1) & (gi == n_group - 1)
    last_y = (ys == width - 1) & (mi == n_member - 1)
    cf[AX] = jnp.where(last_x, 0.0, q * wx)
    cf[AX_LOW] = q * wx_low
    cf[AY] = jnp.where(last_y, 0.0, q * wy)
    cf[AY_LOW] = q * wy_low
    cf[Q] = q
    cf[Q_INV] = diagf * (1.0 / OMEGA)

    def scale(x, carry):
        fetch(x).wait()
        value = rhs[x] * row(Q, x)
        b[x + 1] = value
        return pack(x, value, carry)

    store_columns(0, lax.fori_loop(0, rows, scale, empty, unroll=2))
    first = exchange(0, b)
    lax.fori_loop(early, blocks, pairs, 0)

    def dot_high(left, right):
        return jnp.dot(
            left, right, precision=lax.Precision.HIGHEST, preferred_element_type=F32
        )

    lab = lax.broadcasted_iota(jnp.int32, (rows, LANES), 1)

    def hot_column(column):
        return jnp.where(column == lab, 1.0, 0.0)

    first_hot = hot_column(agg_ref[:, 0:1])
    last_hot = hot_column(agg_ref[:, width - 1:])
    below_hot = hot_column(below_a_ref[:, LANES - 1:])
    above_hot = hot_column(above_a_ref[:, 0:1])
    above = jnp.where(mi < n_member - 1, face_ref[1, :, width - 1:], 0.0)
    half = acc[:, :AGG] + acc[:, AGG:]
    half = half + dot_high(first_hot.T, first_hot * (0.5 * below))
    own = label == row(LABEL, 0)
    low_sum = jnp.sum(jnp.where(own, low_row, 0.0), axis=1, keepdims=True)
    eye = lax.broadcasted_iota(jnp.int32, (AGG, AGG), 0)
    eye = eye == lax.broadcasted_iota(jnp.int32, (AGG, AGG), 1)
    half = half + jnp.where(eye, 0.5 * low_sum, 0.0)
    w = jnp.concatenate(
        [
            half + half.T,
            -dot_high(below_hot.T, first_hot * below),
            -dot_high(above_hot.T, last_hot * above),
        ],
        axis=0,
    )
    lm = jnp.sum(jnp.abs(w), axis=0, keepdims=True)
    lm_send[...] = jnp.broadcast_to(lm, lm_send.shape)
    lm_copies = []
    for off in range(1, n_member):
        peer = lax.rem(mi + off, n_member)
        copy = remote(
            lm_send, lm_recv.at[off - 1], lm_ssem.at[off - 1], lm_rsem.at[off - 1], (gi, peer)
        )
        copy.start()
        lm_copies.append(copy)
    w_high, w_low = split(w)

    def pre(x):
        cur, total = neighbours(b, x)
        return (2.0 - OMEGA) * cur + total

    store_columns(1, sweep(0, first, pre, f, 1, 2))
    second = exchange(1, f)

    def restrict(x, carry):
        cur, total = neighbours(f, x)
        resid = (b[x + 1] - OMEGA * cur + total) * row(Q_INV, x)
        high, low = split(resid)
        both = jnp.concatenate([high, low], axis=0)
        return carry + lax.dot_general(both, hot_of(x), NT, preferred_element_type=F32)

    sums = lax.fori_loop(
        1, rows - 1, restrict, jnp.zeros((2 * n_rhs, AGG), F32), unroll=2
    )
    finish(second)
    sums = restrict(rows - 1, restrict(0, sums))
    resid = sums[:n_rhs] + sums[n_rhs:]
    resid = resid + dot_high(
        pltpu.roll(col_recv[1, 0], LANES - 1, 1)[:, :rows], first_hot * below
    )
    resid = resid + dot_high(col_recv[1, 1][:, :rows], last_hot * above)

    finish(lm_copies)
    lm8 = lm_send[...]
    for off in range(1, n_member):
        lm8 = jnp.maximum(lm8, lm_recv[off - 1])
    lmax = jnp.max(lm8[0:1], axis=1, keepdims=True)
    lmin = lmax / RATIO
    theta = (lmax + lmin) / 2.0
    delta = (lmax - lmin) / 2.0
    sigma = theta / delta
    rho = 1.0 / sigma
    direc = resid / theta
    sol = jnp.zeros_like(resid)
    for step in range(CHEB):
        if step + 1 < CHEB:
            dir_send[step] = direc
            copies = [
                remote(
                    dir_send.at[step], dir_recv.at[step, i],
                    dir_ssem.at[step, i], dir_rsem.at[step, i], (gi, peer),
                )
                for i, peer in enumerate((m_up, m_down))
            ]
            for copy in copies:
                copy.start()
            sol = sol + direc
            rho_new = 1.0 / (2.0 * sigma - rho)
            finish(copies)
            vec = jnp.concatenate([direc, dir_recv[step, 0], dir_recv[step, 1]], axis=1)
            v_high, v_low = split(vec)
            both = jnp.concatenate([v_high, v_low], axis=0)
            prod = jnp.dot(both, w_high, preferred_element_type=F32)
            prod = prod[:n_rhs] + prod[n_rhs:]
            prod = prod + jnp.dot(v_high, w_low, preferred_element_type=F32)
            resid = resid - prod
            direc = rho_new * rho * direc + (2.0 * rho_new / delta) * resid
            rho = rho_new
        else:
            sol = sol + direc

    e_high, e_low = split(sol)
    e_both = jnp.concatenate([e_high, e_low], axis=0)

    def prolong(x, carry):
        spread = jnp.dot(e_both, hot_of(x), preferred_element_type=F32)
        value = f[x + 1] + spread[:n_rhs] + spread[n_rhs:]
        g[x + 1] = value
        return pack(x, value, carry)

    store_columns(2, lax.fori_loop(0, rows, prolong, empty, unroll=4))
    third = exchange(2, g)

    def post(x):
        cur, total = neighbours(g, x)
        return b[x + 1] + (1.0 - OMEGA) * cur + total

    store_columns(3, sweep(2, third, post, h, 1, 2))
    fourth = exchange(3, h)

    def final(x):
        cur, total = neighbours(h, x)
        return b[x + 1] + (1.0 - OMEGA) * cur + total

    sweep(3, fourth, final, out_ref, 0, 2)
    for copy in started:
        copy.wait_send()


def local(right_side, diagonal, face_weight, aggregation):
    n_group, n_member = lax.axis_size("group"), lax.axis_size("member")
    n_rhs, rows, width = right_side.shape
    padded = pltpu.VMEM((rows + 2, n_rhs, width), F32)
    dma = pltpu.SemaphoreType.DMA
    vmem = pl.BlockSpec(memory_space=pltpu.VMEM)
    out = pl.pallas_call(
        functools.partial(cycle_kernel, n_group, n_member),
        out_shape=jax.ShapeDtypeStruct((rows, n_rhs, width), F32),
        in_specs=[pl.BlockSpec(memory_space=pl.ANY), vmem, vmem, vmem],
        out_specs=vmem,
        scratch_shapes=[
            pltpu.VMEM((rows, n_rhs, width), F32),
            pltpu.VMEM((12, rows, width), F32),
            pltpu.VMEM((AGG, 2 * AGG), F32),
            pltpu.VMEM((8, width), F32),
            pltpu.VMEM((rows, LANES), F32),
            pltpu.VMEM((rows, LANES), jnp.int32),
            pltpu.VMEM((rows, LANES), jnp.int32),
            padded, padded, padded, padded,
            pltpu.VMEM((4, 2, n_rhs, LANES), F32),
            pltpu.VMEM((4, 2, n_rhs, LANES), F32),
            pltpu.VMEM((CHEB - 1, n_rhs, AGG), F32),
            pltpu.VMEM((CHEB - 1, 2, n_rhs, AGG), F32),
            pltpu.VMEM((8, AGG), F32),
            pltpu.VMEM((n_member - 1, 8, AGG), F32),
            dma((rows,)), dma((4,)), dma((4,)),
            dma((4, 4)), dma((4, 4)),
            dma((CHEB - 1, 2)), dma((CHEB - 1, 2)),
            dma((n_member - 1,)), dma((n_member - 1,)),
        ],
        compiler_params=pltpu.CompilerParams(
            collective_id=0, has_side_effects=True, vmem_limit_bytes=48 * 1024 * 1024
        ),
    )(right_side, diagonal, face_weight, aggregation)
    return out.transpose(1, 0, 2)


def solution(mesh):
    placed = (
        P(None, "group", "member"),
        P("group", "member"),
        P(None, "group", "member"),
        P("group", "member"),
    )
    return jax.shard_map(
        local, mesh=mesh, in_specs=placed, out_specs=P(None, "group", "member"), check_vma=False
    )
```

```python
import functools

import jax
import jax.numpy as jnp
from jax import lax
from jax.experimental import pallas as pl
from jax.experimental.pallas import tpu as pltpu
from jax.sharding import PartitionSpec as P

AGG = 128
POST = 2
CHEB = 6
OMEGA = 0.8
RATIO = 30.0
LANES = 128
MESH = pl.DeviceIdType.MESH
F32 = jnp.float32
BF16 = jnp.bfloat16
NT = (((1,), (1,)), ((), ()))


def split(value):
    high = value.astype(BF16)
    return high, (value - high.astype(F32)).astype(BF16)


AX, AX_LOW, AY, AY_LOW, Q, Q_INV, LABEL, LABEL_X, LABEL_Y, WX, WY, HALF = range(12)
D_BLOCK = 4
NEAR = (-2, -1, 1, 2)
FAR = (-3, -2, -1, 1, 2, 3)


def cycle_kernel(
    n_group, n_member, rhs_hbm, diag_ref, face_ref, agg_ref, out_ref,
    rhs, cf, acc, low_row_ref, below_w_ref, below_a_ref, above_a_ref,
    b, f, g, h, col_send, col_recv, dir_send, dir_recv, lm_send, lm_recv,
    w_send, w_recv, state_send, state_recv,
    rhs_sem, w_ssem, w_rsem, state_ssem, state_rsem, edge_ssem, edge_rsem, halo_ssem, halo_rsem, dir_ssem, dir_rsem, lm_ssem, lm_rsem,
):
    rows, n_rhs, width = rhs.shape
    tiles = width // LANES
    gi = lax.axis_index("group")
    mi = lax.axis_index("member")
    g_up, g_down = lax.rem(gi + 1, n_group), lax.rem(gi + n_group - 1, n_group)
    m_up, m_down = lax.rem(mi + 1, n_member), lax.rem(mi + n_member - 1, n_member)

    def member_at(off):
        return lax.rem(mi + off + n_member, n_member)

    def fetch(x):
        return pltpu.make_async_copy(rhs_hbm.at[:, x, :], rhs.at[x], rhs_sem.at[x])

    def start_fetch(x, carry):
        fetch(x).start()
        return carry

    lax.fori_loop(0, rows, start_fetch, 0)

    barrier = pltpu.get_barrier_semaphore()
    for peer in (g_up, g_down):
        pl.semaphore_signal(barrier, inc=1, device_id=(peer, mi), device_id_type=MESH)
    for off in range(1, n_member):
        peer = lax.rem(mi + off, n_member)
        pl.semaphore_signal(barrier, inc=1, device_id=(gi, peer), device_id_type=MESH)

    lane = lax.broadcasted_iota(jnp.int32, (n_rhs, LANES), 1)
    label = lax.broadcasted_iota(jnp.int32, (AGG, width), 0).astype(F32)

    def remote(src, dst, ssem, rsem, target):
        return pltpu.make_async_remote_copy(
            src_ref=src, dst_ref=dst, send_sem=ssem, recv_sem=rsem,
            device_id=target, device_id_type=MESH,
        )

    def exchange(phase, buf):
        plan = (
            (buf.at[rows], buf.at[0], (g_up, mi)),
            (buf.at[1], buf.at[rows + 1], (g_down, mi)),
            (col_send.at[phase, 0], col_recv.at[phase, 0], (gi, m_up)),
            (col_send.at[phase, 1], col_recv.at[phase, 1], (gi, m_down)),
        )
        copies = [
            remote(s, d, halo_ssem.at[phase, i], halo_rsem.at[phase, i], t)
            for i, (s, d, t) in enumerate(plan)
        ]
        for copy in copies:
            copy.start()
        return copies

    started = []

    def finish(copies):
        for copy in copies:
            copy.wait_recv()
        started.extend(copies)

    def pack(x, value, carry):
        last, first = carry
        last = jnp.where(lane == x + 1, pltpu.roll(value[:, value.shape[1] - LANES:], x + 2, 1), last)
        first = jnp.where(lane == x, pltpu.roll(value[:, :LANES], x, 1), first)
        return last, first

    def store_columns(phase, carry):
        col_send[phase, 0] = carry[0]
        col_send[phase, 1] = carry[1]

    empty = (jnp.zeros((n_rhs, LANES), F32), jnp.zeros((n_rhs, LANES), F32))

    def neighbours(buf, x):
        cur = buf[x + 1]
        parts = [cur[:, k * LANES:(k + 1) * LANES] for k in range(tiles)]
        zero = jnp.zeros((n_rhs, LANES), F32)
        right = [zero] + [pltpu.roll(p, 1, 1) for p in parts]
        left = [pltpu.roll(p, LANES - 1, 1) for p in parts] + [zero]
        low = [jnp.where(lane == 0, right[k], right[k + 1]) for k in range(tiles)]
        high = [jnp.where(lane == LANES - 1, left[k + 1], left[k]) for k in range(tiles)]
        low = jnp.concatenate(low, axis=1)
        high = jnp.concatenate(high, axis=1)
        total = cf[AX, pl.ds(x, 1), :] * buf[x + 2] + cf[AX_LOW, pl.ds(x, 1), :] * buf[x]
        return cur, total + cf[AY, pl.ds(x, 1), :] * high + cf[AY_LOW, pl.ds(x, 1), :] * low

    def patch(phase, x):
        before = pltpu.roll(col_recv[phase, 0], 127 - x, 1)
        after = pltpu.roll(col_recv[phase, 1], 127 - x, 1)
        low = jnp.where(lane == 0, before, 0.0) * cf[AY_LOW, pl.ds(x, 1), :][:, :LANES]
        high = jnp.where(lane == LANES - 1, after, 0.0) * cf[AY, pl.ds(x, 1), :][:, width - LANES:]
        return low, high

    def sweep(phase, copies, body, dest, shift, unroll):
        def inner(x, carry):
            dest[x + shift] = body(x)
            return carry

        lax.fori_loop(1, rows - 1, inner, 0, unroll=unroll)
        finish(copies)
        inner(0, 0)
        inner(rows - 1, 0)

        def outer(x, carry):
            low, high = patch(phase, x)
            first = dest[x + shift, :, :LANES] + low
            last = dest[x + shift, :, width - LANES:] + high
            dest[x + shift, :, :LANES] = first
            dest[x + shift, :, width - LANES:] = last
            return pack(x, jnp.concatenate([first, last], axis=1), carry)

        return lax.fori_loop(0, rows, outer, empty, unroll=4)

    def row(plane, x):
        return cf[plane, pl.ds(x, 1), :]

    def hot_of(x):
        return jnp.where(label == row(LABEL, x), 1.0, 0.0).astype(BF16)

    wx, wy, agg = face_ref[0], face_ref[1], agg_ref[...].astype(F32)
    xs = lax.broadcasted_iota(jnp.int32, (rows, width), 0)
    ys = lax.broadcasted_iota(jnp.int32, (rows, width), 1)
    wx_low = jnp.where(xs == 0, 0.0, pltpu.roll(wx, 1, 0))
    wy_low = jnp.where(ys == 0, 0.0, pltpu.roll(wy, 1, 1))
    own_diag = diag_ref[...] + wx + wy + wx_low + wy_low
    cf[LABEL] = agg
    cf[LABEL_X] = pltpu.roll(agg, rows - 1, 0)
    cf[LABEL_Y] = pltpu.roll(agg, width - 1, 1)
    cf[WX] = jnp.where(xs == rows - 1, 0.0, wx)
    cf[WY] = jnp.where(ys == width - 1, 0.0, wy)
    cf[HALF] = 0.5 * own_diag
    acc[...] = jnp.zeros_like(acc)

    pl.semaphore_wait(barrier, n_member + 1)
    edges = [
        remote(s, d, edge_ssem.at[i], edge_rsem.at[i], t)
        for i, (s, d, t) in enumerate((
            (face_ref.at[0, pl.ds(rows - 8, 8), :], low_row_ref, (g_up, mi)),
            (face_ref.at[1, :, pl.ds(width - LANES, LANES)], below_w_ref, (gi, m_up)),
            (agg_ref.at[:, pl.ds(width - LANES, LANES)], below_a_ref, (gi, m_up)),
            (agg_ref.at[:, pl.ds(0, LANES)], above_a_ref, (gi, m_down)),
        ))
    ]
    for copy in edges:
        copy.start()

    def pairs(block, carry):
        total = jnp.zeros(acc.shape, F32)
        for i in range(D_BLOCK):
            x = block * D_BLOCK + i
            own = label == row(LABEL, x)
            hot = jnp.where(own, 1.0, 0.0).astype(BF16)
            value = jnp.where(own, row(HALF, x), 0.0)
            value = value - jnp.where(label == row(LABEL_X, x), row(WX, x), 0.0)
            value = value - jnp.where(label == row(LABEL_Y, x), row(WY, x), 0.0)
            high, low = split(value)
            both = jnp.concatenate([high, low], axis=0)
            total = total + lax.dot_general(hot, both, NT, preferred_element_type=F32)
        acc[...] += total
        return carry

    blocks = rows // D_BLOCK
    early = blocks * 5 // 8
    lax.fori_loop(0, early, pairs, 0)
    finish(edges)

    low_row = jnp.where(gi > 0, low_row_ref[7:8, :], 0.0)
    below = jnp.where(mi > 0, below_w_ref[:, LANES - 1:], 0.0)
    wx_low = wx_low + jnp.where(xs == 0, low_row, 0.0)
    wy_low = wy_low + jnp.where(ys == 0, below, 0.0)
    diagf = diag_ref[...] + wx + wy + wx_low + wy_low
    q = OMEGA / diagf
    last_x = (xs == rows - 1) & (gi == n_group - 1)
    last_y = (ys == width - 1) & (mi == n_member - 1)
    cf[AX] = jnp.where(last_x, 0.0, q * wx)
    cf[AX_LOW] = q * wx_low
    cf[AY] = jnp.where(last_y, 0.0, q * wy)
    cf[AY_LOW] = q * wy_low
    cf[Q] = q
    cf[Q_INV] = diagf * (1.0 / OMEGA)

    def scale(x, carry):
        fetch(x).wait()
        value = rhs[x] * row(Q, x)
        b[x + 1] = value
        return pack(x, value, carry)

    store_columns(0, lax.fori_loop(0, rows, scale, empty, unroll=2))
    first = exchange(0, b)
    lax.fori_loop(early, blocks, pairs, 0)

    def dot_high(left, right):
        return jnp.dot(
            left, right, precision=lax.Precision.HIGHEST, preferred_element_type=F32
        )

    lab = lax.broadcasted_iota(jnp.int32, (rows, LANES), 1)

    def hot_column(column):
        return jnp.where(column == lab, 1.0, 0.0)

    first_hot = hot_column(agg_ref[:, 0:1])
    last_hot = hot_column(agg_ref[:, width - 1:])
    below_hot = hot_column(below_a_ref[:, LANES - 1:])
    above_hot = hot_column(above_a_ref[:, 0:1])
    above = jnp.where(mi < n_member - 1, face_ref[1, :, width - 1:], 0.0)
    half = acc[:, :AGG] + acc[:, AGG:]
    half = half + dot_high(first_hot.T, first_hot * (0.5 * below))
    own = label == row(LABEL, 0)
    low_sum = jnp.sum(jnp.where(own, low_row, 0.0), axis=1, keepdims=True)
    eye = lax.broadcasted_iota(jnp.int32, (AGG, AGG), 0)
    eye = eye == lax.broadcasted_iota(jnp.int32, (AGG, AGG), 1)
    half = half + jnp.where(eye, 0.5 * low_sum, 0.0)
    w = jnp.concatenate(
        [
            half + half.T,
            -dot_high(below_hot.T, first_hot * below),
            -dot_high(above_hot.T, last_hot * above),
        ],
        axis=0,
    )
    lm = jnp.sum(jnp.abs(w), axis=0, keepdims=True)
    lm_send[...] = jnp.broadcast_to(lm, lm_send.shape)
    lm_copies = []
    for off in range(1, n_member):
        peer = lax.rem(mi + off, n_member)
        copy = remote(
            lm_send, lm_recv.at[off - 1], lm_ssem.at[off - 1], lm_rsem.at[off - 1], (gi, peer)
        )
        copy.start()
        lm_copies.append(copy)
    w_send[...] = w
    w_copies = {}
    for i, off in enumerate(NEAR):
        w_copies[-off] = (i, remote(
            w_send, w_recv.at[i], w_ssem.at[i], w_rsem.at[i], (gi, member_at(off))
        ))
        w_copies[-off][1].start()

    def pre(x):
        cur, total = neighbours(b, x)
        return (2.0 - OMEGA) * cur + total

    store_columns(1, sweep(0, first, pre, f, 1, 2))
    second = exchange(1, f)

    def restrict(x, carry):
        cur, total = neighbours(f, x)
        resid = (b[x + 1] - OMEGA * cur + total) * row(Q_INV, x)
        high, low = split(resid)
        both = jnp.concatenate([high, low], axis=0)
        return carry + lax.dot_general(both, hot_of(x), NT, preferred_element_type=F32)

    sums = lax.fori_loop(
        1, rows - 1, restrict, jnp.zeros((2 * n_rhs, AGG), F32), unroll=2
    )
    finish(second)
    sums = restrict(rows - 1, restrict(0, sums))
    resid = sums[:n_rhs] + sums[n_rhs:]
    resid = resid + dot_high(
        pltpu.roll(col_recv[1, 0], LANES - 1, 1)[:, :rows], first_hot * below
    )
    resid = resid + dot_high(col_recv[1, 1][:, :rows], last_hot * above)

    finish(lm_copies)
    lm8 = lm_send[...]
    for off in range(1, n_member):
        lm8 = jnp.maximum(lm8, lm_recv[off - 1])
    lmax = jnp.max(lm8[0:1], axis=1, keepdims=True)
    lmin = lmax / RATIO
    theta = (lmax + lmin) / 2.0
    delta = (lmax - lmin) / 2.0
    sigma = theta / delta
    rho = 1.0 / sigma
    finish([copy for _, copy in w_copies.values()])
    blocks_w = {0: split(w_send[...])}
    for off, (i, _) in w_copies.items():
        blocks_w[off] = split(w_recv[i])

    def product(at, dirs):
        w_high, w_low = blocks_w[at]
        vec = jnp.concatenate([dirs[at], dirs[at - 1], dirs[at + 1]], axis=1)
        v_high, v_low = split(vec)
        both = jnp.concatenate([v_high, v_low], axis=0)
        prod = jnp.dot(both, w_high, preferred_element_type=F32)
        prod = prod[:n_rhs] + prod[n_rhs:]
        return prod + jnp.dot(v_high, w_low, preferred_element_type=F32)

    def gather(send, recv, ssem, rsem, offsets):
        copies = [
            remote(send, recv.at[i], ssem.at[i], rsem.at[i], (gi, member_at(off)))
            for i, off in enumerate(offsets)
        ]
        for copy in copies:
            copy.start()
        finish(copies)

    dirs = {0: resid / theta}
    dir_send[...] = dirs[0]
    gather(dir_send, dir_recv, dir_ssem, dir_rsem, FAR)
    res = {0: resid}
    for i, off in enumerate(FAR):
        dirs[-off] = dir_recv[i]
        res[-off] = dirs[-off] * theta
    reach = 3
    sol = jnp.zeros_like(resid)
    for step in range(CHEB):
        sol = sol + dirs[0]
        if step + 1 < CHEB:
            if reach == 0:
                state_send[0] = dirs[0]
                state_send[1] = res[0]
                gather(state_send, state_recv, state_ssem, state_rsem, NEAR)
                for i, off in enumerate(NEAR):
                    dirs[-off] = state_recv[i, 0]
                    res[-off] = state_recv[i, 1]
                reach = 2
            reach -= 1
            rho_new = 1.0 / (2.0 * sigma - rho)
            own_scale, res_scale = rho_new * rho, 2.0 * rho_new / delta
            inside = range(-reach, reach + 1)
            res = {at: res[at] - product(at, dirs) for at in inside}
            dirs = {at: own_scale * dirs[at] + res_scale * res[at] for at in inside}
            rho = rho_new

    e_high, e_low = split(sol)
    e_both = jnp.concatenate([e_high, e_low], axis=0)

    def prolong(x, carry):
        spread = jnp.dot(e_both, hot_of(x), preferred_element_type=F32)
        value = f[x + 1] + spread[:n_rhs] + spread[n_rhs:]
        g[x + 1] = value
        return pack(x, value, carry)

    store_columns(2, lax.fori_loop(0, rows, prolong, empty, unroll=4))
    third = exchange(2, g)

    def post(x):
        cur, total = neighbours(g, x)
        return b[x + 1] + (1.0 - OMEGA) * cur + total

    store_columns(3, sweep(2, third, post, h, 1, 2))
    fourth = exchange(3, h)

    def final(x):
        cur, total = neighbours(h, x)
        return b[x + 1] + (1.0 - OMEGA) * cur + total

    sweep(3, fourth, final, out_ref, 0, 2)
    for copy in started:
        copy.wait_send()


def local(right_side, diagonal, face_weight, aggregation):
    n_group, n_member = lax.axis_size("group"), lax.axis_size("member")
    n_rhs, rows, width = right_side.shape
    padded = pltpu.VMEM((rows + 2, n_rhs, width), F32)
    dma = pltpu.SemaphoreType.DMA
    vmem = pl.BlockSpec(memory_space=pltpu.VMEM)
    out = pl.pallas_call(
        functools.partial(cycle_kernel, n_group, n_member),
        out_shape=jax.ShapeDtypeStruct((rows, n_rhs, width), F32),
        in_specs=[pl.BlockSpec(memory_space=pl.ANY), vmem, vmem, vmem],
        out_specs=vmem,
        scratch_shapes=[
            pltpu.VMEM((rows, n_rhs, width), F32),
            pltpu.VMEM((12, rows, width), F32),
            pltpu.VMEM((AGG, 2 * AGG), F32),
            pltpu.VMEM((8, width), F32),
            pltpu.VMEM((rows, LANES), F32),
            pltpu.VMEM((rows, LANES), jnp.int32),
            pltpu.VMEM((rows, LANES), jnp.int32),
            padded, padded, padded, padded,
            pltpu.VMEM((4, 2, n_rhs, LANES), F32),
            pltpu.VMEM((4, 2, n_rhs, LANES), F32),
            pltpu.VMEM((n_rhs, AGG), F32),
            pltpu.VMEM((len(FAR), n_rhs, AGG), F32),
            pltpu.VMEM((8, AGG), F32),
            pltpu.VMEM((n_member - 1, 8, AGG), F32),
            pltpu.VMEM((3 * AGG, AGG), F32),
            pltpu.VMEM((len(NEAR), 3 * AGG, AGG), F32),
            pltpu.VMEM((2, n_rhs, AGG), F32),
            pltpu.VMEM((len(NEAR), 2, n_rhs, AGG), F32),
            dma((rows,)), dma((len(NEAR),)), dma((len(NEAR),)),
            dma((len(NEAR),)), dma((len(NEAR),)), dma((4,)), dma((4,)),
            dma((4, 4)), dma((4, 4)),
            dma((len(FAR),)), dma((len(FAR),)),
            dma((n_member - 1,)), dma((n_member - 1,)),
        ],
        compiler_params=pltpu.CompilerParams(
            collective_id=0, has_side_effects=True, vmem_limit_bytes=48 * 1024 * 1024
        ),
    )(right_side, diagonal, face_weight, aggregation)
    return out.transpose(1, 0, 2)


def solution(mesh):
    placed = (
        P(None, "group", "member"),
        P("group", "member"),
        P(None, "group", "member"),
        P("group", "member"),
    )
    return jax.shard_map(
        local, mesh=mesh, in_specs=placed, out_specs=P(None, "group", "member"), check_vma=False
    )
```

```python
import functools

import jax
import jax.numpy as jnp
from jax import lax
from jax.experimental import pallas as pl
from jax.experimental.pallas import tpu as pltpu
from jax.sharding import PartitionSpec as P

AGG = 128
POST = 2
CHEB = 6
OMEGA = 0.8
RATIO = 30.0
LANES = 128
MESH = pl.DeviceIdType.MESH
F32 = jnp.float32
BF16 = jnp.bfloat16
NT = (((1,), (1,)), ((), ()))


def split(value):
    high = value.astype(BF16)
    return high, (value - high.astype(F32)).astype(BF16)


AX, AX_LOW, AY, AY_LOW, Q, Q_INV, LABEL, LABEL_X, LABEL_Y, WX, WY, HALF = range(12)
D_BLOCK = 4
NEAR = (-2, -1, 1, 2)
FAR = (-3, -2, -1, 1, 2, 3)


def cycle_kernel(
    n_group, n_member, rhs_hbm, diag_hbm, face_hbm, agg_hbm, out_hbm,
    diag_ref, face_ref, agg_ref, in_sem, out_sem, rhs, cf, acc, low_row_ref, below_w_ref, below_a_ref, above_a_ref,
    b, f, g, h, col_send, col_recv, dir_send, dir_recv, lm_send, lm_recv,
    w_send, w_recv, state_send, state_recv,
    rhs_sem, w_ssem, w_rsem, state_ssem, state_rsem, edge_ssem, edge_rsem, halo_ssem, halo_rsem, dir_ssem, dir_rsem, lm_ssem, lm_rsem,
):
    rows, n_rhs, width = rhs.shape
    tiles = width // LANES
    gi = lax.axis_index("group")
    mi = lax.axis_index("member")
    g_up, g_down = lax.rem(gi + 1, n_group), lax.rem(gi + n_group - 1, n_group)
    m_up, m_down = lax.rem(mi + 1, n_member), lax.rem(mi + n_member - 1, n_member)

    def member_at(off):
        return lax.rem(mi + off + n_member, n_member)

    def fetch(x):
        return pltpu.make_async_copy(rhs_hbm.at[:, x, :], rhs.at[x], rhs_sem.at[x])

    def start_fetch(x, carry):
        fetch(x).start()
        return carry

    inputs = [
        pltpu.make_async_copy(s, d, in_sem.at[i])
        for i, (s, d) in enumerate(
            ((agg_hbm, agg_ref), (face_hbm, face_ref), (diag_hbm, diag_ref))
        )
    ]
    for copy in inputs:
        copy.start()
    lax.fori_loop(0, rows, start_fetch, 0)

    barrier = pltpu.get_barrier_semaphore()
    for peer in (g_up, g_down):
        pl.semaphore_signal(barrier, inc=1, device_id=(peer, mi), device_id_type=MESH)
    for off in range(1, n_member):
        peer = lax.rem(mi + off, n_member)
        pl.semaphore_signal(barrier, inc=1, device_id=(gi, peer), device_id_type=MESH)

    lane = lax.broadcasted_iota(jnp.int32, (n_rhs, LANES), 1)
    label = lax.broadcasted_iota(jnp.int32, (AGG, width), 0).astype(F32)

    def remote(src, dst, ssem, rsem, target):
        return pltpu.make_async_remote_copy(
            src_ref=src, dst_ref=dst, send_sem=ssem, recv_sem=rsem,
            device_id=target, device_id_type=MESH,
        )

    def exchange(phase, buf):
        plan = (
            (buf.at[rows], buf.at[0], (g_up, mi)),
            (buf.at[1], buf.at[rows + 1], (g_down, mi)),
            (col_send.at[phase, 0], col_recv.at[phase, 0], (gi, m_up)),
            (col_send.at[phase, 1], col_recv.at[phase, 1], (gi, m_down)),
        )
        copies = [
            remote(s, d, halo_ssem.at[phase, i], halo_rsem.at[phase, i], t)
            for i, (s, d, t) in enumerate(plan)
        ]
        for copy in copies:
            copy.start()
        return copies

    started = []

    def finish(copies):
        for copy in copies:
            copy.wait_recv()
        started.extend(copies)

    def pack(x, value, carry):
        last, first = carry
        last = jnp.where(lane == x + 1, pltpu.roll(value[:, value.shape[1] - LANES:], x + 2, 1), last)
        first = jnp.where(lane == x, pltpu.roll(value[:, :LANES], x, 1), first)
        return last, first

    def store_columns(phase, carry):
        col_send[phase, 0] = carry[0]
        col_send[phase, 1] = carry[1]

    empty = (jnp.zeros((n_rhs, LANES), F32), jnp.zeros((n_rhs, LANES), F32))

    def neighbours(buf, x):
        cur = buf[x + 1]
        parts = [cur[:, k * LANES:(k + 1) * LANES] for k in range(tiles)]
        zero = jnp.zeros((n_rhs, LANES), F32)
        right = [zero] + [pltpu.roll(p, 1, 1) for p in parts]
        left = [pltpu.roll(p, LANES - 1, 1) for p in parts] + [zero]
        low = [jnp.where(lane == 0, right[k], right[k + 1]) for k in range(tiles)]
        high = [jnp.where(lane == LANES - 1, left[k + 1], left[k]) for k in range(tiles)]
        low = jnp.concatenate(low, axis=1)
        high = jnp.concatenate(high, axis=1)
        total = cf[AX, pl.ds(x, 1), :] * buf[x + 2] + cf[AX_LOW, pl.ds(x, 1), :] * buf[x]
        return cur, total + cf[AY, pl.ds(x, 1), :] * high + cf[AY_LOW, pl.ds(x, 1), :] * low

    def patch(phase, x):
        before = pltpu.roll(col_recv[phase, 0], 127 - x, 1)
        after = pltpu.roll(col_recv[phase, 1], 127 - x, 1)
        low = jnp.where(lane == 0, before, 0.0) * cf[AY_LOW, pl.ds(x, 1), :][:, :LANES]
        high = jnp.where(lane == LANES - 1, after, 0.0) * cf[AY, pl.ds(x, 1), :][:, width - LANES:]
        return low, high

    def sweep(phase, copies, body, dest, shift, unroll, done=None):
        def inner(x, carry):
            dest[x + shift] = body(x)
            return carry

        lax.fori_loop(1, rows - 1, inner, 0, unroll=unroll)
        finish(copies)
        inner(0, 0)
        inner(rows - 1, 0)

        def outer(x, carry):
            low, high = patch(phase, x)
            first = dest[x + shift, :, :LANES] + low
            last = dest[x + shift, :, width - LANES:] + high
            dest[x + shift, :, :LANES] = first
            dest[x + shift, :, width - LANES:] = last
            if done is not None:
                done(x)
                return carry
            return pack(x, jnp.concatenate([first, last], axis=1), carry)

        return lax.fori_loop(0, rows, outer, empty, unroll=4)

    def row(plane, x):
        return cf[plane, pl.ds(x, 1), :]

    def hot_of(x):
        return jnp.where(label == row(LABEL, x), 1.0, 0.0).astype(BF16)

    for copy in inputs:
        copy.wait()

    wx, wy, agg = face_ref[0], face_ref[1], agg_ref[...].astype(F32)
    xs = lax.broadcasted_iota(jnp.int32, (rows, width), 0)
    ys = lax.broadcasted_iota(jnp.int32, (rows, width), 1)
    wx_low = jnp.where(xs == 0, 0.0, pltpu.roll(wx, 1, 0))
    wy_low = jnp.where(ys == 0, 0.0, pltpu.roll(wy, 1, 1))
    own_diag = diag_ref[...] + wx + wy + wx_low + wy_low
    cf[LABEL] = agg
    cf[LABEL_X] = pltpu.roll(agg, rows - 1, 0)
    cf[LABEL_Y] = pltpu.roll(agg, width - 1, 1)
    cf[WX] = jnp.where(xs == rows - 1, 0.0, wx)
    cf[WY] = jnp.where(ys == width - 1, 0.0, wy)
    cf[HALF] = 0.5 * own_diag
    acc[...] = jnp.zeros_like(acc)

    pl.semaphore_wait(barrier, n_member + 1)
    edges = [
        remote(s, d, edge_ssem.at[i], edge_rsem.at[i], t)
        for i, (s, d, t) in enumerate((
            (face_ref.at[0, pl.ds(rows - 8, 8), :], low_row_ref, (g_up, mi)),
            (face_ref.at[1, :, pl.ds(width - LANES, LANES)], below_w_ref, (gi, m_up)),
            (agg_ref.at[:, pl.ds(width - LANES, LANES)], below_a_ref, (gi, m_up)),
            (agg_ref.at[:, pl.ds(0, LANES)], above_a_ref, (gi, m_down)),
        ))
    ]
    for copy in edges:
        copy.start()

    def pairs(block, carry):
        total = jnp.zeros(acc.shape, F32)
        for i in range(D_BLOCK):
            x = block * D_BLOCK + i
            own = label == row(LABEL, x)
            hot = jnp.where(own, 1.0, 0.0).astype(BF16)
            value = jnp.where(own, row(HALF, x), 0.0)
            value = value - jnp.where(label == row(LABEL_X, x), row(WX, x), 0.0)
            value = value - jnp.where(label == row(LABEL_Y, x), row(WY, x), 0.0)
            high, low = split(value)
            both = jnp.concatenate([high, low], axis=0)
            total = total + lax.dot_general(hot, both, NT, preferred_element_type=F32)
        acc[...] += total
        return carry

    blocks = rows // D_BLOCK
    lax.fori_loop(0, blocks, pairs, 0)
    finish(edges)

    low_row = jnp.where(gi > 0, low_row_ref[7:8, :], 0.0)
    below = jnp.where(mi > 0, below_w_ref[:, LANES - 1:], 0.0)
    wx_low = wx_low + jnp.where(xs == 0, low_row, 0.0)
    wy_low = wy_low + jnp.where(ys == 0, below, 0.0)
    diagf = diag_ref[...] + wx + wy + wx_low + wy_low
    q = OMEGA / diagf
    last_x = (xs == rows - 1) & (gi == n_group - 1)
    last_y = (ys == width - 1) & (mi == n_member - 1)
    cf[AX] = jnp.where(last_x, 0.0, q * wx)
    cf[AX_LOW] = q * wx_low
    cf[AY] = jnp.where(last_y, 0.0, q * wy)
    cf[AY_LOW] = q * wy_low
    cf[Q] = q
    cf[Q_INV] = diagf * (1.0 / OMEGA)

    def scale(x, carry):
        fetch(x).wait()
        value = rhs[x] * row(Q, x)
        b[x + 1] = value
        return pack(x, value, carry)

    store_columns(0, lax.fori_loop(0, rows, scale, empty, unroll=2))
    first = exchange(0, b)

    def dot_high(left, right):
        return jnp.dot(
            left, right, precision=lax.Precision.HIGHEST, preferred_element_type=F32
        )

    lab = lax.broadcasted_iota(jnp.int32, (rows, LANES), 1)

    def hot_column(column):
        return jnp.where(column == lab, 1.0, 0.0)

    first_hot = hot_column(agg_ref[:, 0:1])
    last_hot = hot_column(agg_ref[:, width - 1:])
    below_hot = hot_column(below_a_ref[:, LANES - 1:])
    above_hot = hot_column(above_a_ref[:, 0:1])
    above = jnp.where(mi < n_member - 1, face_ref[1, :, width - 1:], 0.0)
    half = acc[:, :AGG] + acc[:, AGG:]
    half = half + dot_high(first_hot.T, first_hot * (0.5 * below))
    own = label == row(LABEL, 0)
    low_sum = jnp.sum(jnp.where(own, low_row, 0.0), axis=1, keepdims=True)
    eye = lax.broadcasted_iota(jnp.int32, (AGG, AGG), 0)
    eye = eye == lax.broadcasted_iota(jnp.int32, (AGG, AGG), 1)
    half = half + jnp.where(eye, 0.5 * low_sum, 0.0)
    w = jnp.concatenate(
        [
            half + half.T,
            -dot_high(below_hot.T, first_hot * below),
            -dot_high(above_hot.T, last_hot * above),
        ],
        axis=0,
    )
    lm = jnp.sum(jnp.abs(w), axis=0, keepdims=True)
    lm_send[...] = jnp.broadcast_to(lm, lm_send.shape)
    lm_copies = []
    for off in range(1, n_member):
        peer = lax.rem(mi + off, n_member)
        copy = remote(
            lm_send, lm_recv.at[off - 1], lm_ssem.at[off - 1], lm_rsem.at[off - 1], (gi, peer)
        )
        copy.start()
        lm_copies.append(copy)
    w_send[...] = w
    w_copies = {}
    for i, off in enumerate(NEAR):
        w_copies[-off] = (i, remote(
            w_send, w_recv.at[i], w_ssem.at[i], w_rsem.at[i], (gi, member_at(off))
        ))
        w_copies[-off][1].start()

    def pre(x):
        cur, total = neighbours(b, x)
        return (2.0 - OMEGA) * cur + total

    store_columns(1, sweep(0, first, pre, f, 1, 2))
    second = exchange(1, f)

    def restrict(x, carry):
        cur, total = neighbours(f, x)
        resid = (b[x + 1] - OMEGA * cur + total) * row(Q_INV, x)
        high, low = split(resid)
        both = jnp.concatenate([high, low], axis=0)
        return carry + lax.dot_general(both, hot_of(x), NT, preferred_element_type=F32)

    sums = lax.fori_loop(
        1, rows - 1, restrict, jnp.zeros((2 * n_rhs, AGG), F32), unroll=2
    )
    finish(second)
    sums = restrict(rows - 1, restrict(0, sums))
    resid = sums[:n_rhs] + sums[n_rhs:]
    resid = resid + dot_high(
        pltpu.roll(col_recv[1, 0], LANES - 1, 1)[:, :rows], first_hot * below
    )
    resid = resid + dot_high(col_recv[1, 1][:, :rows], last_hot * above)

    finish(lm_copies)
    lm8 = lm_send[...]
    for off in range(1, n_member):
        lm8 = jnp.maximum(lm8, lm_recv[off - 1])
    lmax = jnp.max(lm8[0:1], axis=1, keepdims=True)
    lmin = lmax / RATIO
    theta = (lmax + lmin) / 2.0
    delta = (lmax - lmin) / 2.0
    sigma = theta / delta
    rho = 1.0 / sigma
    finish([copy for _, copy in w_copies.values()])
    blocks_w = {0: split(w_send[...])}
    for off, (i, _) in w_copies.items():
        blocks_w[off] = split(w_recv[i])

    def product(at, dirs):
        w_high, w_low = blocks_w[at]
        vec = jnp.concatenate([dirs[at], dirs[at - 1], dirs[at + 1]], axis=1)
        v_high, v_low = split(vec)
        both = jnp.concatenate([v_high, v_low], axis=0)
        prod = jnp.dot(both, w_high, preferred_element_type=F32)
        prod = prod[:n_rhs] + prod[n_rhs:]
        return prod + jnp.dot(v_high, w_low, preferred_element_type=F32)

    def gather(send, recv, ssem, rsem, offsets):
        copies = [
            remote(send, recv.at[i], ssem.at[i], rsem.at[i], (gi, member_at(off)))
            for i, off in enumerate(offsets)
        ]
        for copy in copies:
            copy.start()
        finish(copies)

    dirs = {0: resid / theta}
    dir_send[...] = dirs[0]
    gather(dir_send, dir_recv, dir_ssem, dir_rsem, FAR)
    res = {0: resid}
    for i, off in enumerate(FAR):
        dirs[-off] = dir_recv[i]
        res[-off] = dirs[-off] * theta
    reach = 3
    sol = jnp.zeros_like(resid)
    for step in range(CHEB):
        sol = sol + dirs[0]
        if step + 1 < CHEB:
            if reach == 0:
                state_send[0] = dirs[0]
                state_send[1] = res[0]
                gather(state_send, state_recv, state_ssem, state_rsem, NEAR)
                for i, off in enumerate(NEAR):
                    dirs[-off] = state_recv[i, 0]
                    res[-off] = state_recv[i, 1]
                reach = 2
            reach -= 1
            rho_new = 1.0 / (2.0 * sigma - rho)
            own_scale, res_scale = rho_new * rho, 2.0 * rho_new / delta
            inside = range(-reach, reach + 1)
            res = {at: res[at] - product(at, dirs) for at in inside}
            dirs = {at: own_scale * dirs[at] + res_scale * res[at] for at in inside}
            rho = rho_new

    e_high, e_low = split(sol)
    e_both = jnp.concatenate([e_high, e_low], axis=0)

    def prolong(x, carry):
        spread = jnp.dot(e_both, hot_of(x), preferred_element_type=F32)
        value = f[x + 1] + spread[:n_rhs] + spread[n_rhs:]
        g[x + 1] = value
        return pack(x, value, carry)

    store_columns(2, lax.fori_loop(0, rows, prolong, empty, unroll=4))
    third = exchange(2, g)

    def post(x):
        cur, total = neighbours(g, x)
        return b[x + 1] + (1.0 - OMEGA) * cur + total

    store_columns(3, sweep(2, third, post, h, 1, 2))
    fourth = exchange(3, h)

    def final(x):
        cur, total = neighbours(h, x)
        return b[x + 1] + (1.0 - OMEGA) * cur + total

    def result(x):
        return pltpu.make_async_copy(rhs.at[x], out_hbm.at[x], out_sem.at[x])

    sweep(3, fourth, final, rhs, 0, 2, lambda x: result(x).start())

    def wait_result(x, carry):
        result(x).wait()
        return carry

    lax.fori_loop(0, rows, wait_result, 0)
    for copy in started:
        copy.wait_send()


def local(right_side, diagonal, face_weight, aggregation):
    n_group, n_member = lax.axis_size("group"), lax.axis_size("member")
    n_rhs, rows, width = right_side.shape
    padded = pltpu.VMEM((rows + 2, n_rhs, width), F32)
    dma = pltpu.SemaphoreType.DMA
    anywhere = pl.BlockSpec(memory_space=pl.ANY)
    out = pl.pallas_call(
        functools.partial(cycle_kernel, n_group, n_member),
        out_shape=jax.ShapeDtypeStruct((rows, n_rhs, width), F32),
        in_specs=[anywhere] * 4,
        out_specs=anywhere,
        scratch_shapes=[
            pltpu.VMEM((rows, width), F32),
            pltpu.VMEM((2, rows, width), F32),
            pltpu.VMEM((rows, width), jnp.int32),
            dma((3,)), dma((rows,)),
            pltpu.VMEM((rows, n_rhs, width), F32),
            pltpu.VMEM((12, rows, width), F32),
            pltpu.VMEM((AGG, 2 * AGG), F32),
            pltpu.VMEM((8, width), F32),
            pltpu.VMEM((rows, LANES), F32),
            pltpu.VMEM((rows, LANES), jnp.int32),
            pltpu.VMEM((rows, LANES), jnp.int32),
            padded, padded, padded, padded,
            pltpu.VMEM((4, 2, n_rhs, LANES), F32),
            pltpu.VMEM((4, 2, n_rhs, LANES), F32),
            pltpu.VMEM((n_rhs, AGG), F32),
            pltpu.VMEM((len(FAR), n_rhs, AGG), F32),
            pltpu.VMEM((8, AGG), F32),
            pltpu.VMEM((n_member - 1, 8, AGG), F32),
            pltpu.VMEM((3 * AGG, AGG), F32),
            pltpu.VMEM((len(NEAR), 3 * AGG, AGG), F32),
            pltpu.VMEM((2, n_rhs, AGG), F32),
            pltpu.VMEM((len(NEAR), 2, n_rhs, AGG), F32),
            dma((rows,)), dma((len(NEAR),)), dma((len(NEAR),)),
            dma((len(NEAR),)), dma((len(NEAR),)), dma((4,)), dma((4,)),
            dma((4, 4)), dma((4, 4)),
            dma((len(FAR),)), dma((len(FAR),)),
            dma((n_member - 1,)), dma((n_member - 1,)),
        ],
        compiler_params=pltpu.CompilerParams(
            collective_id=0, has_side_effects=True, vmem_limit_bytes=60 * 1024 * 1024
        ),
    )(right_side, diagonal, face_weight, aggregation)
    return out.transpose(1, 0, 2)


def solution(mesh):
    placed = (
        P(None, "group", "member"),
        P("group", "member"),
        P(None, "group", "member"),
        P("group", "member"),
    )
    return jax.shard_map(
        local, mesh=mesh, in_specs=placed, out_specs=P(None, "group", "member"), check_vma=False
    )
```

```python
import functools

import jax
import jax.numpy as jnp
from jax import lax
from jax.experimental import pallas as pl
from jax.experimental.pallas import tpu as pltpu
from jax.sharding import PartitionSpec as P

AGG = 128
POST = 2
CHEB = 6
OMEGA = 0.8
RATIO = 30.0
LANES = 128
MESH = pl.DeviceIdType.MESH
F32 = jnp.float32
BF16 = jnp.bfloat16
NT = (((1,), (1,)), ((), ()))


def split(value):
    high = value.astype(BF16)
    return high, (value - high.astype(F32)).astype(BF16)


AX, AX_LOW, AY, AY_LOW, Q, Q_INV, LABEL, LABEL_X, LABEL_Y, WX, WY, HALF = range(12)
D_BLOCK = 4
NEAR = (-2, -1, 1, 2)
FAR = (-3, -2, -1, 1, 2, 3)


def cycle_kernel(
    n_group, n_member, rhs_hbm, diag_ref, face_ref, agg_ref, out_ref,
    rhs, cf, acc, low_row_ref, below_w_ref, below_a_ref, above_a_ref,
    b, f, g, h, col_send, col_recv, dir_send, dir_recv, lm_send, lm_recv,
    w_send, w_recv, state_send, state_recv,
    rhs_sem, w_ssem, w_rsem, state_ssem, state_rsem, edge_ssem, edge_rsem, halo_ssem, halo_rsem, dir_ssem, dir_rsem, lm_ssem, lm_rsem,
):
    rows, n_rhs, width = rhs.shape
    tiles = width // LANES
    gi = lax.axis_index("group")
    mi = lax.axis_index("member")
    g_up, g_down = lax.rem(gi + 1, n_group), lax.rem(gi + n_group - 1, n_group)
    m_up, m_down = lax.rem(mi + 1, n_member), lax.rem(mi + n_member - 1, n_member)

    def member_at(off):
        return lax.rem(mi + off + n_member, n_member)

    def fetch(x):
        return pltpu.make_async_copy(rhs_hbm.at[:, x, :], rhs.at[x], rhs_sem.at[x])

    def start_fetch(x, carry):
        fetch(x).start()
        return carry

    lax.fori_loop(0, rows, start_fetch, 0)

    barrier = pltpu.get_barrier_semaphore()
    for peer in (g_up, g_down):
        pl.semaphore_signal(barrier, inc=1, device_id=(peer, mi), device_id_type=MESH)
    for off in range(1, n_member):
        peer = lax.rem(mi + off, n_member)
        pl.semaphore_signal(barrier, inc=1, device_id=(gi, peer), device_id_type=MESH)

    lane = lax.broadcasted_iota(jnp.int32, (n_rhs, LANES), 1)
    label = lax.broadcasted_iota(jnp.int32, (AGG, width), 0).astype(F32)

    def remote(src, dst, ssem, rsem, target):
        return pltpu.make_async_remote_copy(
            src_ref=src, dst_ref=dst, send_sem=ssem, recv_sem=rsem,
            device_id=target, device_id_type=MESH,
        )

    def exchange(phase, buf):
        plan = (
            (buf.at[rows], buf.at[0], (g_up, mi)),
            (buf.at[1], buf.at[rows + 1], (g_down, mi)),
            (col_send.at[phase, 0], col_recv.at[phase, 0], (gi, m_up)),
            (col_send.at[phase, 1], col_recv.at[phase, 1], (gi, m_down)),
        )
        copies = [
            remote(s, d, halo_ssem.at[phase, i], halo_rsem.at[phase, i], t)
            for i, (s, d, t) in enumerate(plan)
        ]
        for copy in copies:
            copy.start()
        return copies

    started = []

    def finish(copies):
        for copy in copies:
            copy.wait_recv()
        started.extend(copies)

    def pack(x, value, carry):
        last, first = carry
        last = jnp.where(lane == x + 1, pltpu.roll(value[:, value.shape[1] - LANES:], x + 2, 1), last)
        first = jnp.where(lane == x, pltpu.roll(value[:, :LANES], x, 1), first)
        return last, first

    def store_columns(phase, carry):
        col_send[phase, 0] = carry[0]
        col_send[phase, 1] = carry[1]

    empty = (jnp.zeros((n_rhs, LANES), F32), jnp.zeros((n_rhs, LANES), F32))

    def neighbours(buf, x):
        cur = buf[x + 1]
        parts = [cur[:, k * LANES:(k + 1) * LANES] for k in range(tiles)]
        zero = jnp.zeros((n_rhs, LANES), F32)
        right = [zero] + [pltpu.roll(p, 1, 1) for p in parts]
        left = [pltpu.roll(p, LANES - 1, 1) for p in parts] + [zero]
        low = [jnp.where(lane == 0, right[k], right[k + 1]) for k in range(tiles)]
        high = [jnp.where(lane == LANES - 1, left[k + 1], left[k]) for k in range(tiles)]
        low = jnp.concatenate(low, axis=1)
        high = jnp.concatenate(high, axis=1)
        total = cf[AX, pl.ds(x, 1), :] * buf[x + 2] + cf[AX_LOW, pl.ds(x, 1), :] * buf[x]
        return cur, total + cf[AY, pl.ds(x, 1), :] * high + cf[AY_LOW, pl.ds(x, 1), :] * low

    def patch(phase, x):
        before = pltpu.roll(col_recv[phase, 0], 127 - x, 1)
        after = pltpu.roll(col_recv[phase, 1], 127 - x, 1)
        low = jnp.where(lane == 0, before, 0.0) * cf[AY_LOW, pl.ds(x, 1), :][:, :LANES]
        high = jnp.where(lane == LANES - 1, after, 0.0) * cf[AY, pl.ds(x, 1), :][:, width - LANES:]
        return low, high

    def sweep(phase, copies, body, dest, shift, unroll):
        def inner(x, carry):
            dest[x + shift] = body(x)
            return carry

        lax.fori_loop(1, rows - 1, inner, 0, unroll=unroll)
        finish(copies)
        inner(0, 0)
        inner(rows - 1, 0)

        def outer(x, carry):
            low, high = patch(phase, x)
            first = dest[x + shift, :, :LANES] + low
            last = dest[x + shift, :, width - LANES:] + high
            dest[x + shift, :, :LANES] = first
            dest[x + shift, :, width - LANES:] = last
            return pack(x, jnp.concatenate([first, last], axis=1), carry)

        return lax.fori_loop(0, rows, outer, empty, unroll=4)

    def row(plane, x):
        return cf[plane, pl.ds(x, 1), :]

    def hot_of(x):
        return jnp.where(label == row(LABEL, x), 1.0, 0.0).astype(BF16)

    wx, wy, agg = face_ref[0], face_ref[1], agg_ref[...].astype(F32)
    xs = lax.broadcasted_iota(jnp.int32, (rows, width), 0)
    ys = lax.broadcasted_iota(jnp.int32, (rows, width), 1)
    wx_low = jnp.where(xs == 0, 0.0, pltpu.roll(wx, 1, 0))
    wy_low = jnp.where(ys == 0, 0.0, pltpu.roll(wy, 1, 1))
    own_diag = diag_ref[...] + wx + wy + wx_low + wy_low
    cf[LABEL] = agg
    cf[LABEL_X] = pltpu.roll(agg, rows - 1, 0)
    cf[LABEL_Y] = pltpu.roll(agg, width - 1, 1)
    cf[WX] = jnp.where(xs == rows - 1, 0.0, wx)
    cf[WY] = jnp.where(ys == width - 1, 0.0, wy)
    cf[HALF] = 0.5 * own_diag
    acc[...] = jnp.zeros_like(acc)

    pl.semaphore_wait(barrier, n_member + 1)
    edges = [
        remote(s, d, edge_ssem.at[i], edge_rsem.at[i], t)
        for i, (s, d, t) in enumerate((
            (face_ref.at[0, pl.ds(rows - 8, 8), :], low_row_ref, (g_up, mi)),
            (face_ref.at[1, :, pl.ds(width - LANES, LANES)], below_w_ref, (gi, m_up)),
            (agg_ref.at[:, pl.ds(width - LANES, LANES)], below_a_ref, (gi, m_up)),
            (agg_ref.at[:, pl.ds(0, LANES)], above_a_ref, (gi, m_down)),
        ))
    ]
    for copy in edges:
        copy.start()

    def pairs(block, carry):
        total = jnp.zeros(acc.shape, F32)
        for i in range(D_BLOCK):
            x = block * D_BLOCK + i
            own = label == row(LABEL, x)
            hot = jnp.where(own, 1.0, 0.0).astype(BF16)
            value = jnp.where(own, row(HALF, x), 0.0)
            value = value - jnp.where(label == row(LABEL_X, x), row(WX, x), 0.0)
            value = value - jnp.where(label == row(LABEL_Y, x), row(WY, x), 0.0)
            high, low = split(value)
            both = jnp.concatenate([high, low], axis=0)
            total = total + lax.dot_general(hot, both, NT, preferred_element_type=F32)
        acc[...] += total
        return carry

    blocks = rows // D_BLOCK
    early = blocks
    lax.fori_loop(0, early, pairs, 0)
    finish(edges)

    low_row = jnp.where(gi > 0, low_row_ref[7:8, :], 0.0)
    below = jnp.where(mi > 0, below_w_ref[:, LANES - 1:], 0.0)
    wx_low = wx_low + jnp.where(xs == 0, low_row, 0.0)
    wy_low = wy_low + jnp.where(ys == 0, below, 0.0)
    diagf = diag_ref[...] + wx + wy + wx_low + wy_low
    q = OMEGA / diagf
    last_x = (xs == rows - 1) & (gi == n_group - 1)
    last_y = (ys == width - 1) & (mi == n_member - 1)
    cf[AX] = jnp.where(last_x, 0.0, q * wx)
    cf[AX_LOW] = q * wx_low
    cf[AY] = jnp.where(last_y, 0.0, q * wy)
    cf[AY_LOW] = q * wy_low
    cf[Q] = q
    cf[Q_INV] = diagf * (1.0 / OMEGA)

    def scale(x, carry):
        fetch(x).wait()
        value = rhs[x] * row(Q, x)
        b[x + 1] = value
        return pack(x, value, carry)

    store_columns(0, lax.fori_loop(0, rows, scale, empty, unroll=2))
    first = exchange(0, b)
    lax.fori_loop(early, blocks, pairs, 0)

    def dot_high(left, right):
        return jnp.dot(
            left, right, precision=lax.Precision.HIGHEST, preferred_element_type=F32
        )

    lab = lax.broadcasted_iota(jnp.int32, (rows, LANES), 1)

    def hot_column(column):
        return jnp.where(column == lab, 1.0, 0.0)

    first_hot = hot_column(agg_ref[:, 0:1])
    last_hot = hot_column(agg_ref[:, width - 1:])
    below_hot = hot_column(below_a_ref[:, LANES - 1:])
    above_hot = hot_column(above_a_ref[:, 0:1])
    above = jnp.where(mi < n_member - 1, face_ref[1, :, width - 1:], 0.0)
    half = acc[:, :AGG] + acc[:, AGG:]
    half = half + dot_high(first_hot.T, first_hot * (0.5 * below))
    own = label == row(LABEL, 0)
    low_sum = jnp.sum(jnp.where(own, low_row, 0.0), axis=1, keepdims=True)
    eye = lax.broadcasted_iota(jnp.int32, (AGG, AGG), 0)
    eye = eye == lax.broadcasted_iota(jnp.int32, (AGG, AGG), 1)
    half = half + jnp.where(eye, 0.5 * low_sum, 0.0)
    w = jnp.concatenate(
        [
            half + half.T,
            -dot_high(below_hot.T, first_hot * below),
            -dot_high(above_hot.T, last_hot * above),
        ],
        axis=0,
    )
    lm = jnp.sum(jnp.abs(w), axis=0, keepdims=True)
    lm_send[...] = jnp.broadcast_to(lm, lm_send.shape)
    lm_copies = []
    for off in range(1, n_member):
        peer = lax.rem(mi + off, n_member)
        copy = remote(
            lm_send, lm_recv.at[off - 1], lm_ssem.at[off - 1], lm_rsem.at[off - 1], (gi, peer)
        )
        copy.start()
        lm_copies.append(copy)
    w_send[...] = w
    w_copies = {}
    for i, off in enumerate(NEAR):
        w_copies[-off] = (i, remote(
            w_send, w_recv.at[i], w_ssem.at[i], w_rsem.at[i], (gi, member_at(off))
        ))
        w_copies[-off][1].start()

    def pre(x):
        cur, total = neighbours(b, x)
        return (2.0 - OMEGA) * cur + total

    store_columns(1, sweep(0, first, pre, f, 1, 2))
    second = exchange(1, f)

    def restrict(x, carry):
        cur, total = neighbours(f, x)
        resid = (b[x + 1] - OMEGA * cur + total) * row(Q_INV, x)
        high, low = split(resid)
        both = jnp.concatenate([high, low], axis=0)
        return carry + lax.dot_general(both, hot_of(x), NT, preferred_element_type=F32)

    sums = lax.fori_loop(
        1, rows - 1, restrict, jnp.zeros((2 * n_rhs, AGG), F32), unroll=4
    )
    finish(second)
    sums = restrict(rows - 1, restrict(0, sums))
    resid = sums[:n_rhs] + sums[n_rhs:]
    resid = resid + dot_high(
        pltpu.roll(col_recv[1, 0], LANES - 1, 1)[:, :rows], first_hot * below
    )
    resid = resid + dot_high(col_recv[1, 1][:, :rows], last_hot * above)

    finish(lm_copies)
    lm8 = lm_send[...]
    for off in range(1, n_member):
        lm8 = jnp.maximum(lm8, lm_recv[off - 1])
    lmax = jnp.max(lm8[0:1], axis=1, keepdims=True)
    lmin = lmax / RATIO
    theta = (lmax + lmin) / 2.0
    delta = (lmax - lmin) / 2.0
    sigma = theta / delta
    rho = 1.0 / sigma
    finish([copy for _, copy in w_copies.values()])
    blocks_w = {0: split(w_send[...])}
    for off, (i, _) in w_copies.items():
        blocks_w[off] = split(w_recv[i])

    def product(at, dirs):
        w_high, w_low = blocks_w[at]
        vec = jnp.concatenate([dirs[at], dirs[at - 1], dirs[at + 1]], axis=1)
        v_high, v_low = split(vec)
        both = jnp.concatenate([v_high, v_low], axis=0)
        prod = jnp.dot(both, w_high, preferred_element_type=F32)
        prod = prod[:n_rhs] + prod[n_rhs:]
        return prod + jnp.dot(v_high, w_low, preferred_element_type=F32)

    def gather(send, recv, ssem, rsem, offsets):
        copies = [
            remote(send, recv.at[i], ssem.at[i], rsem.at[i], (gi, member_at(off)))
            for i, off in enumerate(offsets)
        ]
        for copy in copies:
            copy.start()
        finish(copies)

    dirs = {0: resid / theta}
    dir_send[...] = dirs[0]
    gather(dir_send, dir_recv, dir_ssem, dir_rsem, FAR)
    res = {0: resid}
    for i, off in enumerate(FAR):
        dirs[-off] = dir_recv[i]
        res[-off] = dirs[-off] * theta
    reach = 3
    sol = jnp.zeros_like(resid)
    for step in range(CHEB):
        sol = sol + dirs[0]
        if step + 1 < CHEB:
            if reach == 0:
                state_send[0] = dirs[0]
                state_send[1] = res[0]
                gather(state_send, state_recv, state_ssem, state_rsem, NEAR)
                for i, off in enumerate(NEAR):
                    dirs[-off] = state_recv[i, 0]
                    res[-off] = state_recv[i, 1]
                reach = 2
            reach -= 1
            rho_new = 1.0 / (2.0 * sigma - rho)
            own_scale, res_scale = rho_new * rho, 2.0 * rho_new / delta
            inside = range(-reach, reach + 1)
            res = {at: res[at] - product(at, dirs) for at in inside}
            dirs = {at: own_scale * dirs[at] + res_scale * res[at] for at in inside}
            rho = rho_new

    e_high, e_low = split(sol)
    e_both = jnp.concatenate([e_high, e_low], axis=0)

    def prolong(x, carry):
        spread = jnp.dot(e_both, hot_of(x), preferred_element_type=F32)
        value = f[x + 1] + spread[:n_rhs] + spread[n_rhs:]
        g[x + 1] = value
        return pack(x, value, carry)

    store_columns(2, lax.fori_loop(0, rows, prolong, empty, unroll=4))
    third = exchange(2, g)

    def post(x):
        cur, total = neighbours(g, x)
        return b[x + 1] + (1.0 - OMEGA) * cur + total

    store_columns(3, sweep(2, third, post, h, 1, 2))
    fourth = exchange(3, h)

    def final(x):
        cur, total = neighbours(h, x)
        return b[x + 1] + (1.0 - OMEGA) * cur + total

    sweep(3, fourth, final, out_ref, 0, 2)
    for copy in started:
        copy.wait_send()


def local(right_side, diagonal, face_weight, aggregation):
    n_group, n_member = lax.axis_size("group"), lax.axis_size("member")
    n_rhs, rows, width = right_side.shape
    padded = pltpu.VMEM((rows + 2, n_rhs, width), F32)
    dma = pltpu.SemaphoreType.DMA
    vmem = pl.BlockSpec(memory_space=pltpu.VMEM)
    out = pl.pallas_call(
        functools.partial(cycle_kernel, n_group, n_member),
        out_shape=jax.ShapeDtypeStruct((rows, n_rhs, width), F32),
        in_specs=[pl.BlockSpec(memory_space=pl.ANY), vmem, vmem, vmem],
        out_specs=vmem,
        scratch_shapes=[
            pltpu.VMEM((rows, n_rhs, width), F32),
            pltpu.VMEM((12, rows, width), F32),
            pltpu.VMEM((AGG, 2 * AGG), F32),
            pltpu.VMEM((8, width), F32),
            pltpu.VMEM((rows, LANES), F32),
            pltpu.VMEM((rows, LANES), jnp.int32),
            pltpu.VMEM((rows, LANES), jnp.int32),
            padded, padded, padded, padded,
            pltpu.VMEM((4, 2, n_rhs, LANES), F32),
            pltpu.VMEM((4, 2, n_rhs, LANES), F32),
            pltpu.VMEM((n_rhs, AGG), F32),
            pltpu.VMEM((len(FAR), n_rhs, AGG), F32),
            pltpu.VMEM((8, AGG), F32),
            pltpu.VMEM((n_member - 1, 8, AGG), F32),
            pltpu.VMEM((3 * AGG, AGG), F32),
            pltpu.VMEM((len(NEAR), 3 * AGG, AGG), F32),
            pltpu.VMEM((2, n_rhs, AGG), F32),
            pltpu.VMEM((len(NEAR), 2, n_rhs, AGG), F32),
            dma((rows,)), dma((len(NEAR),)), dma((len(NEAR),)),
            dma((len(NEAR),)), dma((len(NEAR),)), dma((4,)), dma((4,)),
            dma((4, 4)), dma((4, 4)),
            dma((len(FAR),)), dma((len(FAR),)),
            dma((n_member - 1,)), dma((n_member - 1,)),
        ],
        compiler_params=pltpu.CompilerParams(
            collective_id=0, has_side_effects=True, vmem_limit_bytes=48 * 1024 * 1024
        ),
    )(right_side, diagonal, face_weight, aggregation)
    return out.transpose(1, 0, 2)


def solution(mesh):
    placed = (
        P(None, "group", "member"),
        P("group", "member"),
        P(None, "group", "member"),
        P("group", "member"),
    )
    return jax.shard_map(
        local, mesh=mesh, in_specs=placed, out_specs=P(None, "group", "member"), check_vma=False
    )
```
